32 devices in a mesh: dp: 8 (over y, x, core), tensor: 4 (over z).
Axes of the slice: x: 2, y: 2, z: 4, core: 2. Of those that a mesh axis runs over, the one named last changes fastest.
Arguments:
- inputs: bfloat16 [2048, 1792], P('dp', 'tensor'), may hold values from -6 to 6
- cotangent: bfloat16 [2048, 1792], P('dp', 'tensor'), may hold values from -6 to 6
- documents: int32 [2048], P('dp'), may hold values from -1 to 3, as said below
- gains: bfloat16 [2, 1792], P(None, 'tensor'), may hold values from 0.5 to 1.5
- query_key: bfloat16 [1792, 2, 256], P(None, None, 'tensor'), may hold values from -0.125 to 0.125
- value_gate: bfloat16 [1792, 2, 1792], P(None, None, 'tensor'), may hold values from -0.125 to 0.125
- conv_taps: bfloat16 [4, 1792], P(None, 'tensor'), may hold values from -3 to 3
- output_weight: bfloat16 [1792, 1792], P('tensor'), may hold values from -3 to 3
- gate_up: bfloat16 [1792, 2, 4096], P(None, None, 'tensor'), may hold values from -0.125 to 0.125
- down_weight: bfloat16 [4096, 1792], P('tensor'), may hold values from -0.09375 to 0.09375
- gains_moment: float32 [2, 1792], P(None, 'tensor'), may hold values from -60 to 60
- query_key_moment: float32 [1792, 2, 256], P('dp', None, 'tensor'), may hold values from -60 to 60
- value_gate_moment: float32 [1792, 2, 1792], P('dp', None, 'tensor'), may hold values from -60 to 60
- conv_taps_moment: float32 [4, 1792], P(None, 'tensor'), may hold values from -60 to 60
- output_weight_moment: float32 [1792, 1792], P('tensor', 'dp'), may hold values from -60 to 60
- gate_up_moment: float32 [1792, 2, 4096], P('dp', None, 'tensor'), may hold values from -60 to 60
- down_weight_moment: float32 [4096, 1792], P('tensor', 'dp'), may hold values from -60 to 60
- gains_mean: float32 [2, 1792], P(None, 'tensor'), may hold values from -4 to 4
- probe_lookup_smoothed: float32 [1792, 2, 256], P('dp', None, 'tensor'), may hold values from -0.125 to 0.125
- value_gate_mean: float32 [1792, 2, 1792], P('dp', None, 'tensor'), may hold values from -0.125 to 0.125
- conv_taps_mean: float32 [4, 1792], P(None, 'tensor'), may hold values from -3 to 3
- output_weight_mean: float32 [1792, 1792], P('tensor', 'dp'), may hold values from -3 to 3
- gate_up_mean: float32 [1792, 2, 4096], P('dp', None, 'tensor'), may hold values from -0.125 to 0.125
- down_weight_mean: float32 [4096, 1792], P('tensor', 'dp'), may hold values from -0.09375 to 0.09375
Outputs:
- mixed: bfloat16 [2048, 1792], P('dp', 'tensor')
- input_grad: float32 [2048, 1792], P('dp', 'tensor')
- gains_grad: float32 [2, 1792], P(None, 'tensor')
- query_key_grad: float32 [1792, 2, 256], P('dp', None, 'tensor')
- value_gate_grad: float32 [1792, 2, 1792], P('dp', None, 'tensor')
- conv_taps_grad: float32 [4, 1792], P(None, 'tensor')
- output_weight_grad: float32 [1792, 1792], P('tensor', 'dp')
- gate_up_grad: float32 [1792, 2, 4096], P('dp', None, 'tensor')
- down_weight_grad: float32 [4096, 1792], P('tensor', 'dp')
- gains_change: float32 [2, 1792], P(None, 'tensor')
- query_key_change: float32 [1792, 2, 256], P('dp', None, 'tensor')
- value_gate_change: float32 [1792, 2, 1792], P('dp', None, 'tensor')
- conv_taps_change: float32 [4, 1792], P(None, 'tensor')
- output_weight_change: float32 [1792, 1792], P('tensor', 'dp')
- gate_up_change: float32 [1792, 2, 4096], P('dp', None, 'tensor')
- down_weight_change: float32 [4096, 1792], P('tensor', 'dp')
- gains_momentum: float32 [2, 1792], P(None, 'tensor')
- query_key_momentum: float32 [1792, 2, 256], P('dp', None, 'tensor')
- value_gate_momentum: float32 [1792, 2, 1792], P('dp', None, 'tensor')
- conv_taps_momentum: float32 [4, 1792], P(None, 'tensor')
- output_weight_momentum: float32 [1792, 1792], P('tensor', 'dp')
- gate_up_momentum: float32 [1792, 2, 4096], P('dp', None, 'tensor')
- down_weight_momentum: float32 [4096, 1792], P('tensor', 'dp')
- gains_average: float32 [2, 1792], P(None, 'tensor')
- query_key_average: float32 [1792, 2, 256], P('dp', None, 'tensor')
- value_gate_average: float32 [1792, 2, 1792], P('dp', None, 'tensor')
- conv_taps_average: float32 [4, 1792], P(None, 'tensor')
- output_weight_average: float32 [1792, 1792], P('tensor', 'dp')
- gate_up_average: float32 [1792, 2, 4096], P('dp', None, 'tensor')
- down_weight_average: float32 [4096, 1792], P('tensor', 'dp')
The draws below stay inside these ranges and needn't reach their ends.
Inputs may be any that keep to these rules, and one draw needn't show every extreme that they name: `documents`: within each aligned block of 256 rows the numbers start at 0 and never fall; a document spans at least 64 and at most 256 rows (the last one before padding may be shorter), and the first block holds a single document; each block ends with at least one and fewer than 64 padding rows marked -1, and has no other -1.
All inputs are finite; a program needn't handle non-finite values.
Results may differ from the reference program's by a relative error of at most 0.013.
Values may be sent and summed in bfloat16 or wider, within the bound.
No kernel may reach another device: no remote copies, remote signals or barrier semaphores. Data moves between devices by JAX's collectives and lax.ppermute only.
A program may use at most 192 MiB of HBM per device.

```python
import math
import jax
import jax.numpy as jnp
from jax import lax

D = 1792
H = 16
F = 16
FF = 4096
KERNEL = 4
TOK_DEV = 256
SEQ_MAX = 256
BLOCK = 256
QKW = 256
TOKENS = 2048
N_DP = 8


def draw_documents(key, part):
    block_total = TOKENS // TOK_DEV
    shortest = SEQ_MAX // 4
    slot_count = TOK_DEV // shortest + 1
    key_lengths, key_first, key_padding = jax.random.split(jax.random.fold_in(key, 7), 3)
    lengths = jax.random.randint(key_lengths, (block_total, slot_count), shortest, SEQ_MAX + 1)
    coins = jax.random.randint(key_first, (block_total,), 0, 2)
    coins = coins.at[0].set(1)
    first_length = jnp.where(coins == 1, SEQ_MAX, lengths[:, 0])
    lengths = lengths.at[:, 0].set(first_length)
    lengths = lengths.at[block_total - 1].set(jnp.full((slot_count,), shortest, lengths.dtype))
    ends = jnp.cumsum(lengths, axis=1)
    position = jnp.arange(TOK_DEV)
    numbers = jnp.sum((position[None, :, None] >= ends[:, None, :]).astype(jnp.int32), axis=2)
    padding = jax.random.randint(key_padding, (block_total,), 1, shortest)
    padding = padding.at[block_total - 1].set(1)
    numbers = jnp.where(position[None, :] >= TOK_DEV - padding[:, None], -1, numbers)
    return numbers.reshape(-1).astype(jnp.int32)


def level_of(own_key, dims, cuts, least, largest):
    level, own = 1.0, jax.random.fold_in(own_key, 6)
    for axis_at, shards_of in cuts:
        steps = jnp.exp(jax.random.uniform(jax.random.fold_in(own, axis_at), (shards_of,), jnp.float32, least / len(cuts), largest / len(cuts)))
        level = level * jnp.repeat(steps, dims[axis_at] // shards_of).reshape([-1 if axis == axis_at else 1 for axis in range(len(dims))])
    return level


def centred(key, shape, scale, most, pieces=(), kind=jnp.bfloat16):
    loudness = level_of(key, shape, pieces, -0.22, 0.18) if pieces else 1.0
    values = jax.random.normal(key, shape, jnp.float32) * scale * loudness
    return jnp.minimum(jnp.maximum(values, -most), most).astype(kind)


def setup_inputs(seed: int = 0) -> dict:
    key_list = jax.random.split(jax.random.key(seed), 25)
    inputs = centred(key_list[0], (TOKENS, D), 1.0, 6.0, ((0, 8), (1, 4)))
    cotangent = centred(key_list[1], (TOKENS, D), 1.0, 6.0, ((0, 8), (1, 4)))
    documents = draw_documents(jax.random.fold_in(key_list[24], 71), 0)
    gains = jnp.clip(1.0 + 0.1 * jax.random.normal(key_list[3], (2, D), jnp.float32), 0.5, 1.5).astype(jnp.bfloat16)
    query_key = centred(key_list[4], (D, 2, QKW), D ** -0.5, 0.125, ((2, 4),))
    value_gate = centred(key_list[5], (D, 2, D), D ** -0.5, 0.125, ((2, 4),))
    conv_taps = centred(key_list[6], (KERNEL, D), 0.5, 3.0, ((1, 4),))
    output_weight = centred(key_list[7], (D, D), (max(1, D // 448)) ** -0.5, 3.0, ((0, 4),))
    gate_up = centred(key_list[8], (D, 2, FF), D ** -0.5, 0.125, ((2, 4),))
    down_weight = centred(key_list[9], (FF, D), FF ** -0.5, 0.09375, ((0, 4),))
    gains_moment = centred(key_list[10], (2, D), 10.0, 60.0, ((1, 4),), jnp.float32)
    query_key_moment = centred(key_list[11], (D, 2, QKW), 10.0, 60.0, ((0, 8), (2, 4)), jnp.float32)
    value_gate_moment = centred(key_list[12], (D, 2, D), 10.0, 60.0, ((0, 8), (2, 4)), jnp.float32)
    conv_taps_moment = centred(key_list[13], (KERNEL, D), 10.0, 60.0, ((1, 4),), jnp.float32)
    output_weight_moment = centred(key_list[14], (D, D), 10.0, 60.0, ((0, 4), (1, 8)), jnp.float32)
    gate_up_moment = centred(key_list[15], (D, 2, FF), 10.0, 60.0, ((0, 8), (2, 4)), jnp.float32)
    down_weight_moment = centred(key_list[16], (FF, D), 10.0, 60.0, ((0, 4), (1, 8)), jnp.float32)
    gains_mean = centred(key_list[17], (2, D), 1.0, 4.0, ((1, 4),), jnp.float32)
    probe_lookup_smoothed = centred(key_list[18], (D, 2, QKW), D ** -0.5, 0.125, ((0, 8), (2, 4)), jnp.float32)
    value_gate_mean = centred(key_list[19], (D, 2, D), D ** -0.5, 0.125, ((0, 8), (2, 4)), jnp.float32)
    conv_taps_mean = centred(key_list[20], (KERNEL, D), 0.5, 3.0, ((1, 4),), jnp.float32)
    output_weight_mean = centred(key_list[21], (D, D), (max(1, D // 448)) ** -0.5, 3.0, ((0, 4), (1, 8)), jnp.float32)
    gate_up_mean = centred(key_list[22], (D, 2, FF), D ** -0.5, 0.125, ((0, 8), (2, 4)), jnp.float32)
    down_weight_mean = centred(key_list[23], (FF, D), FF ** -0.5, 0.09375, ((0, 4), (1, 8)), jnp.float32)
    return dict(inputs=inputs, cotangent=cotangent, documents=documents, gains=gains, query_key=query_key, value_gate=value_gate, conv_taps=conv_taps, output_weight=output_weight, gate_up=gate_up, down_weight=down_weight, gains_moment=gains_moment, query_key_moment=query_key_moment, value_gate_moment=value_gate_moment, conv_taps_moment=conv_taps_moment, output_weight_moment=output_weight_moment, gate_up_moment=gate_up_moment, down_weight_moment=down_weight_moment, gains_mean=gains_mean, probe_lookup_smoothed=probe_lookup_smoothed, value_gate_mean=value_gate_mean, conv_taps_mean=conv_taps_mean, output_weight_mean=output_weight_mean, gate_up_mean=gate_up_mean, down_weight_mean=down_weight_mean)


highest_precision = lax.Precision.HIGHEST
epsilon = 1e-06
momentum_decay = 0.9
learning_rate = 0.001
average_rate = 0.1

@jax.custom_vjp
def low(v):
    return lax.optimization_barrier(v.astype(jnp.bfloat16)).astype(jnp.float32)

@jax.custom_vjp
def low_back(v):
    return v

def low_keep(v):
    return (low(v), None)

def low_pass(kept, grad):
    return (grad,)

def back_keep(v):
    return (v, None)

def back_low(kept, grad):
    return (low(grad),)
low.defvjp(low_keep, low_pass)
low_back.defvjp(back_keep, back_low)

def shift_down(source, offset, filler):
    pad_width = [(offset, 0)] + [(0, 0)] * (source.ndim - 1)
    return jnp.pad(source, pad_width, constant_values=filler)[:source.shape[0]]

def convolve(values_pre, tap_weights, documents):
    summed = values_pre * tap_weights[0]
    for offset in range(1, KERNEL):
        same_doc = (shift_down(documents, offset, -2) == documents)[:, None]
        summed = summed + jnp.where(same_doc, shift_down(values_pre, offset, 0.0) * tap_weights[offset], 0.0)
    return summed

def attention(queries, keys, mixed_values, documents):
    tokens = queries.shape[0]
    margin = 2 * BLOCK
    key_pad = jnp.pad(keys, ((margin, 0), (0, 0), (0, 0)))
    value_pad = jnp.pad(mixed_values, ((margin, 0), (0, 0), (0, 0)))
    docs_pad = jnp.pad(documents, (margin, 0), constant_values=-2)
    score_factor_scale = 1.0 / math.sqrt(F)

    def one_block(block_index):
        first = block_index * BLOCK
        query_matrix_rows = lax.dynamic_slice_in_dim(queries, first, BLOCK, 0)
        lookup_lines_array = lax.dynamic_slice_in_dim(key_pad, first, 3 * BLOCK, 0)
        value_rows = lax.dynamic_slice_in_dim(value_pad, first, 3 * BLOCK, 0)
        query_docs = lax.dynamic_slice_in_dim(documents, first, BLOCK, 0)
        key_docs = lax.dynamic_slice_in_dim(docs_pad, first, 3 * BLOCK, 0)
        row_index = first + jnp.arange(BLOCK, dtype=jnp.int32)
        column_index = first - margin + jnp.arange(3 * BLOCK, dtype=jnp.int32)
        allowed = (query_docs[:, None] == key_docs[None, :]) & (column_index[None, :] <= row_index[:, None])
        attention_scores = low_back(jnp.einsum('cyg,jyg->ycj', query_matrix_rows, lookup_lines_array, precision=highest_precision) * score_factor_scale)
        weights = jnp.where(allowed[None], 1.0 + attention_scores + 0.5 * attention_scores * attention_scores, 0.0)
        totals = lax.optimization_barrier(jnp.sum(weights, axis=2, keepdims=True))
        probs = low(weights / totals)
        return jnp.einsum('hqk,khe->qhe', probs, value_rows, precision=highest_precision)
    blocks = lax.map(jax.checkpoint(one_block), jnp.arange(tokens // BLOCK, dtype=jnp.int32))
    return blocks.reshape(tokens, queries.shape[1], mixed_values.shape[2])

def layer(inputs, documents, gains, query_key, value_gate, conv_taps, output_weight, gate_up, down_weight):
    tokens = inputs.shape[0]
    root_one = lax.rsqrt(lax.optimization_barrier(jnp.mean(inputs * inputs, axis=1, keepdims=True)) + epsilon)
    normed = low(inputs * root_one * gains[0])
    projected = low(low_back(jnp.einsum('td,dsf->tsf', normed, query_key, precision=highest_precision)))
    queries = projected[:, 0].reshape(tokens, H, F)
    keys = projected[:, 1].reshape(tokens, H, F)
    mixing = low_back(jnp.einsum('td,dsf->tsf', normed, value_gate, precision=highest_precision))
    values_pre = mixing[:, 0]
    gates = mixing[:, 1]
    mixed_values = low(convolve(values_pre, conv_taps, documents)).reshape(tokens, H, D // H)
    attended = low_back(attention(queries, keys, mixed_values, documents).reshape(tokens, D))
    gated = low(attended * jax.nn.silu(gates))
    branch = low_back(jnp.dot(gated, output_weight, precision=highest_precision))
    hidden = inputs + branch
    root_two = lax.rsqrt(lax.optimization_barrier(jnp.mean(hidden * hidden, axis=1, keepdims=True)) + epsilon)
    normed_two = low(hidden * root_two * gains[1])
    inner = low_back(jnp.einsum('td,dsf->tsf', normed_two, gate_up, precision=highest_precision))
    activation = low(jax.nn.silu(inner[:, 0]) * inner[:, 1])
    feed = low_back(jnp.dot(activation, down_weight, precision=highest_precision))
    return hidden + feed

def advance(grad, weight, moment, average):
    moment_new = momentum_decay * moment + (1.0 - momentum_decay) * grad
    change = -learning_rate * ((1.0 - momentum_decay) * grad + momentum_decay * moment_new)
    average_new = average + average_rate * (weight.astype(jnp.float32) + change - average)
    return (change, moment_new, average_new)

def reference(inputs, cotangent, documents, gains, query_key, value_gate, conv_taps, output_weight, gate_up, down_weight, gains_moment, query_key_moment, value_gate_moment, conv_taps_moment, output_weight_moment, gate_up_moment, down_weight_moment, gains_mean, probe_lookup_smoothed, value_gate_mean, conv_taps_mean, output_weight_mean, gate_up_mean, down_weight_mean):
    params = (gains, query_key, value_gate, conv_taps, output_weight, gate_up, down_weight)
    wide_params = tuple((param.astype(jnp.float32) for param in params))
    masked = jnp.where(documents[:, None] >= 0, cotangent, jnp.zeros_like(cotangent)).astype(jnp.float32)
    shards = (inputs.astype(jnp.float32).reshape(N_DP, TOK_DEV, D), masked.reshape(N_DP, TOK_DEV, D), documents.reshape(N_DP, TOK_DEV))

    def one_shard(summed, shard_item):
        shard_inputs, shard_cot, shard_docs = shard_item

        def apply(source, *weights):
            return layer(source, shard_docs, *weights)
        result, pullback = jax.vjp(apply, shard_inputs, *wide_params)
        grads = pullback(shard_cot)
        summed = tuple((left + right for left, right in zip(summed, grads[1:])))
        return (summed, (result.astype(jnp.bfloat16), grads[0]))
    zeros = tuple((jnp.zeros(param.shape, jnp.float32) for param in params))
    grads, (mixed, input_grad) = lax.scan(one_shard, zeros, shards)
    mixed = mixed.reshape(N_DP * TOK_DEV, D)
    input_grad = input_grad.reshape(N_DP * TOK_DEV, D)
    gains_grad, query_key_grad, value_gate_grad, conv_taps_grad, output_weight_grad, gate_up_grad, down_weight_grad = grads
    gains_change, gains_momentum, gains_average = advance(gains_grad, gains, gains_moment, gains_mean)
    query_key_change, query_key_momentum, query_key_average = advance(query_key_grad, query_key, query_key_moment, probe_lookup_smoothed)
    value_gate_change, value_gate_momentum, value_gate_average = advance(value_gate_grad, value_gate, value_gate_moment, value_gate_mean)
    conv_taps_change, conv_taps_momentum, conv_taps_average = advance(conv_taps_grad, conv_taps, conv_taps_moment, conv_taps_mean)
    output_weight_change, output_weight_momentum, output_weight_average = advance(output_weight_grad, output_weight, output_weight_moment, output_weight_mean)
    gate_up_change, gate_up_momentum, gate_up_average = advance(gate_up_grad, gate_up, gate_up_moment, gate_up_mean)
    down_weight_change, down_weight_momentum, down_weight_average = advance(down_weight_grad, down_weight, down_weight_moment, down_weight_mean)
    return (mixed, input_grad, gains_grad, query_key_grad, value_gate_grad, conv_taps_grad, output_weight_grad, gate_up_grad, down_weight_grad, gains_change, query_key_change, value_gate_change, conv_taps_change, output_weight_change, gate_up_change, down_weight_change, gains_momentum, query_key_momentum, value_gate_momentum, conv_taps_momentum, output_weight_momentum, gate_up_momentum, down_weight_momentum, gains_average, query_key_average, value_gate_average, conv_taps_average, output_weight_average, gate_up_average, down_weight_average)
```

```python
import math

import jax
import jax.numpy as jnp
from jax import lax
from jax.sharding import PartitionSpec as P

H = 16
F = 16
KERNEL = 4
BLOCK = 256


epsilon = 1e-06
momentum_decay = 0.9
learning_rate = 0.001
average_rate = 0.1


def silu_slope(argument):
    logistic_output = jax.nn.sigmoid(argument)
    return logistic_output * (1.0 + argument * (1.0 - logistic_output))


def shift_down(source, offset, filler):
    pad_width = [(offset, 0)] + [(0, 0)] * (source.ndim - 1)
    return jnp.pad(source, pad_width, constant_values=filler)[: source.shape[0]]


def shift_up(source, offset, filler):
    pad_width = [(0, offset)] + [(0, 0)] * (source.ndim - 1)
    return jnp.pad(source, pad_width, constant_values=filler)[offset:]


def convolve(values_pre, tap_weights, documents):
    summed = values_pre * tap_weights[0]
    for offset in range(1, KERNEL):
        same_doc = (shift_down(documents, offset, -2) == documents)[:, None]
        summed = summed + jnp.where(
            same_doc, shift_down(values_pre, offset, 0.0) * tap_weights[offset], 0.0
        )
    return summed


def advance(grad, weight, moment, average):
    moment_new = momentum_decay * moment + (1.0 - momentum_decay) * grad
    change = -learning_rate * ((1.0 - momentum_decay) * grad + momentum_decay * moment_new)
    average_new = average + average_rate * (weight.astype(jnp.float32) + change - average)
    return (change, moment_new, average_new)


def take(source, axis_dim, index):
    return lax.dynamic_index_in_dim(source, index, axis_dim, keepdims=False)


def own_bit(bit):
    return (lax.axis_index("dp") >> bit) & 1


def swap_dp(source, bit):
    count = lax.axis_size("dp")
    return lax.ppermute(source, "dp", [(k, k ^ (1 << bit)) for k in range(count)])


def swap_tensor(source, distance):
    count = lax.axis_size("tensor")
    return lax.ppermute(source, "tensor", [(k, k ^ distance) for k in range(count)])


def gather_features(source):
    count = lax.axis_size("tensor")
    own = lax.axis_index("tensor")
    pieces = [source] + [swap_tensor(source, distance) for distance in range(1, count)]
    stacked = jnp.stack(pieces)
    ordered = jnp.stack([take(stacked, 0, own ^ k) for k in range(count)], axis=1)
    return ordered.reshape(source.shape[0], count * source.shape[1])


def sum_features(partial):
    count = lax.axis_size("tensor")
    own = lax.axis_index("tensor")
    share = partial.shape[1] // count
    rounded = partial.astype(jnp.bfloat16)

    def columns(source, index):
        return lax.dynamic_slice_in_dim(source, index * share, share, 1)

    arrived = [
        swap_tensor(columns(rounded, own ^ distance), distance) for distance in range(1, count)
    ]
    total = columns(partial, own)
    for piece in arrived:
        total = total + piece.astype(jnp.float32)
    return total


def product(left, right):
    lead = left.shape[1:]
    flat = left.reshape(left.shape[0], -1)
    out = lax.dot_general(
        flat, right, (((0,), (0,)), ((), ())), preferred_element_type=jnp.float32
    )
    return out.reshape(*lead, right.shape[1])


def sum_rows(left, right, paths):
    count = lax.axis_size("dp")
    bits = count.bit_length() - 1
    rows = left.shape[1] // count
    grid = left.reshape(left.shape[0], count // 2, 2, rows)
    sent_rows = take(grid, 2, 1 - own_bit(0))
    kept_rows = take(grid, 2, own_bit(0))
    columns = right.shape[1]
    if paths == 2:
        middle = -(-columns // 256) * 128
        parts = (right[:, :middle], right[:, middle:])
        orders = (tuple(range(1, bits)), tuple(reversed(range(1, bits))))
    else:
        parts = (right,)
        orders = (tuple(range(1, bits)),)
    results = []
    for part, order in zip(parts, orders):
        arrived = swap_dp(product(sent_rows, part).astype(jnp.bfloat16), 0)
        shape = (2,) * (bits - 1)
        kept = kept_rows.reshape(kept_rows.shape[0], *shape, rows)
        arrived = arrived.reshape(*shape, rows, part.shape[1])
        remaining = list(reversed(range(1, bits)))
        bit = order[0]
        at = remaining.index(bit)

        def partial(which):
            picked = product(take(kept, at + 1, which), part)
            return picked + take(arrived, at, which).astype(jnp.float32)

        received = swap_dp(partial(1 - own_bit(bit)).astype(jnp.bfloat16), bit)
        total = partial(own_bit(bit)) + received.astype(jnp.float32)
        remaining.pop(at)
        for bit in order[1:]:
            at = remaining.index(bit)
            received = swap_dp(take(total, at, 1 - own_bit(bit)).astype(jnp.bfloat16), bit)
            total = take(total, at, own_bit(bit)) + received.astype(jnp.float32)
            remaining.pop(at)
        results.append(total)
    return results[0] if paths == 1 else jnp.concatenate(results, axis=1)


def sum_dp(source):
    for bit in range(lax.axis_size("dp").bit_length() - 1):
        source = source + swap_dp(source, bit)
    return source


def local(
    inputs,
    cotangent,
    documents,
    gains,
    query_key,
    value_gate,
    conv_taps,
    output_weight,
    gate_up,
    down_weight,
    gains_moment,
    query_key_moment,
    value_gate_moment,
    conv_taps_moment,
    output_weight_moment,
    gate_up_moment,
    down_weight_moment,
    gains_mean,
    probe_lookup_smoothed,
    value_gate_mean,
    conv_taps_mean,
    output_weight_mean,
    gate_up_mean,
    down_weight_mean,
):
    tokens = inputs.shape[0]
    feature_share = inputs.shape[1]
    groups = lax.axis_size("tensor")
    model_width = feature_share * groups
    local_heads = H // groups
    head_size = model_width // H
    score_factor_scale = 1.0 / math.sqrt(F)
    own_start = lax.axis_index("tensor") * feature_share

    def own_columns(source):
        return lax.dynamic_slice_in_dim(source, own_start, feature_share, source.ndim - 1)

    packed = jnp.concatenate([inputs, jnp.pad(gains, ((0, 14), (0, 0)))], axis=0)
    packed_whole = lax.all_gather(packed, "tensor", axis=1, tiled=True)
    whole_inputs = packed_whole[:tokens]
    whole_gains = packed_whole[tokens : tokens + 2]
    masked = jnp.where(documents[:, None] >= 0, cotangent, jnp.zeros_like(cotangent))
    masked, packed_whole = lax.optimization_barrier((masked, packed_whole))
    cot_whole = gather_features(masked)
    inputs_wide = whole_inputs.astype(jnp.float32)
    gain_one = whole_gains[0].astype(jnp.float32)
    gain_two = whole_gains[1].astype(jnp.float32)
    root_one = lax.rsqrt(jnp.mean(inputs_wide * inputs_wide, axis=1, keepdims=True) + epsilon)
    unit_one = inputs_wide * root_one
    normed = (unit_one * gain_one).astype(jnp.bfloat16)
    projected = jnp.einsum(
        "td,dsf->tsf", normed, query_key, preferred_element_type=jnp.float32
    ).astype(jnp.bfloat16)
    queries = projected[:, 0].reshape(tokens, local_heads, F)
    keys = projected[:, 1].reshape(tokens, local_heads, F)
    mixing = jnp.einsum("td,dsf->tsf", normed, value_gate, preferred_element_type=jnp.float32)
    values_pre = mixing[:, 0]
    gates = mixing[:, 1]
    tap_weights = conv_taps.astype(jnp.float32)
    mixed_values = (
        convolve(values_pre, tap_weights, documents)
        .astype(jnp.bfloat16)
        .reshape(tokens, local_heads, head_size)
    )
    margin = 2 * BLOCK
    key_pad = jnp.pad(keys, ((margin, 0), (0, 0), (0, 0)))
    value_pad = jnp.pad(mixed_values, ((margin, 0), (0, 0), (0, 0)))
    docs_pad = jnp.pad(documents, (margin, 0), constant_values=-2)
    block_count = tokens // BLOCK

    def window(block_index):
        first = block_index * BLOCK
        row_index = first + jnp.arange(BLOCK, dtype=jnp.int32)
        column_index = first - margin + jnp.arange(3 * BLOCK, dtype=jnp.int32)
        allowed = (documents[:, None] == docs_pad[None, :]) & (
            column_index[None, :] <= row_index[:, None]
        )
        attention_scores = (
            jnp.einsum("cyg,jyg->ycj", queries, key_pad, preferred_element_type=jnp.float32)
            * score_factor_scale
        )
        weights = jnp.where(
            allowed[None], 1.0 + attention_scores + 0.5 * attention_scores * attention_scores, 0.0
        )
        return (queries, key_pad, value_pad, allowed, attention_scores, weights)

    def forward_block(block_index):
        query_matrix_rows, lookup_lines_array, value_rows, allowed, attention_scores, weights = (
            window(block_index)
        )
        totals = jnp.sum(weights, axis=2)
        probs = (weights / totals[:, :, None]).astype(jnp.bfloat16)
        result = jnp.einsum("hqk,khe->qhe", probs, value_rows, preferred_element_type=jnp.float32)
        return (result, totals)

    attended, kept_totals = lax.map(forward_block, jnp.arange(block_count, dtype=jnp.int32))
    attended = attended.reshape(tokens, feature_share)
    gate_silu = jax.nn.silu(gates)
    gated = (attended * gate_silu).astype(jnp.bfloat16)
    branch_own = sum_features(jnp.dot(gated, output_weight, preferred_element_type=jnp.float32))
    hidden_own = inputs.astype(jnp.float32) + branch_own
    hidden = lax.all_gather(
        hidden_own.astype(jnp.bfloat16), "tensor", axis=1, tiled=True
    ).astype(jnp.float32)
    root_two = lax.rsqrt(jnp.mean(hidden * hidden, axis=1, keepdims=True) + epsilon)
    unit_two = hidden * root_two
    normed_two = (unit_two * gain_two).astype(jnp.bfloat16)
    inner = jnp.einsum("td,dsf->tsf", normed_two, gate_up, preferred_element_type=jnp.float32)
    opener_before_squash = inner[:, 0]
    up_pre = inner[:, 1]
    unit_silu = jax.nn.silu(opener_before_squash)
    activation = (unit_silu * up_pre).astype(jnp.bfloat16)
    feed_partial = jnp.dot(activation, down_weight, preferred_element_type=jnp.float32)
    down_grad_rows = sum_rows(cot_whole, activation, 2)
    d_act = jnp.einsum("td,fd->tf", cot_whole, down_weight, preferred_element_type=jnp.float32)
    d_inner = jnp.stack(
        [d_act * up_pre * silu_slope(opener_before_squash), d_act * unit_silu], axis=1
    ).astype(jnp.bfloat16)
    d_normed_two_own = sum_features(
        jnp.einsum("tsf,dsf->td", d_inner, gate_up, preferred_element_type=jnp.float32)
    )
    gate_up_grad = sum_rows(normed_two, d_inner.reshape(tokens, -1), 2).reshape(
        -1, 2, gate_up.shape[2]
    )
    d_normed_two = lax.all_gather(
        d_normed_two_own.astype(jnp.bfloat16), "tensor", axis=1, tiled=True
    ).astype(jnp.float32)
    scaled_two = d_normed_two * gain_two
    gain_two_grad = jnp.sum(d_normed_two_own * own_columns(unit_two), axis=0)
    d_hidden = cot_whole.astype(jnp.float32) + root_two * (
        scaled_two - unit_two * jnp.mean(scaled_two * unit_two, axis=1, keepdims=True)
    )
    d_branch = d_hidden.astype(jnp.bfloat16)
    output_grad_rows = sum_rows(d_branch, gated, 1)
    feed_own = sum_features(feed_partial)
    mixed = (hidden_own + feed_own).astype(jnp.bfloat16)
    d_gated = jnp.einsum("td,cd->tc", d_branch, output_weight, preferred_element_type=jnp.float32)
    d_attended = (d_gated * gate_silu).astype(jnp.bfloat16).reshape(tokens, local_heads, head_size)
    d_gates = (d_gated * attended * silu_slope(gates)).astype(jnp.bfloat16)

    def backward_block(carry, block_index):
        key_acc, payload_accumulator = carry
        query_matrix_rows, lookup_lines_array, value_rows, allowed, attention_scores, weights = (
            window(block_index)
        )
        totals = kept_totals[block_index]
        probs = weights / totals[:, :, None]
        first = block_index * BLOCK
        value_part = jnp.einsum(
            "hqk,qhe->khe",
            probs.astype(jnp.bfloat16),
            d_attended,
            preferred_element_type=jnp.float32,
        )
        d_probs = jnp.einsum(
            "qhe,khe->hqk", d_attended, value_rows, preferred_element_type=jnp.float32
        )
        d_weights = (d_probs - jnp.sum(d_probs * probs, axis=2, keepdims=True)) / totals[:, :, None]
        logit_slope_delta = jnp.where(
            allowed[None], d_weights * (1.0 + attention_scores), 0.0
        ).astype(jnp.bfloat16)
        query_part = (
            jnp.einsum(
                "ogw,wox->gox",
                logit_slope_delta,
                lookup_lines_array,
                preferred_element_type=jnp.float32,
            )
            * score_factor_scale
        )
        key_part = (
            jnp.einsum(
                "naj,ano->jno",
                logit_slope_delta,
                query_matrix_rows,
                preferred_element_type=jnp.float32,
            )
            * score_factor_scale
        )
        key_acc = key_acc + key_part
        payload_accumulator = payload_accumulator + value_part
        return ((key_acc, payload_accumulator), query_part)

    start_carry = (
        jnp.zeros((tokens + margin, local_heads, F), jnp.float32),
        jnp.zeros((tokens + margin, local_heads, head_size), jnp.float32),
    )
    (key_acc, payload_accumulator), query_parts = lax.scan(
        backward_block, start_carry, jnp.arange(block_count, dtype=jnp.int32)
    )
    d_queries = query_parts.reshape(tokens, local_heads * F).astype(jnp.bfloat16)
    d_keys = key_acc[margin:].reshape(tokens, local_heads * F).astype(jnp.bfloat16)
    d_mixed = payload_accumulator[margin:].reshape(tokens, feature_share)
    d_values = d_mixed * tap_weights[0]
    tap_rows = [jnp.sum(d_mixed * values_pre, axis=0)]
    for offset in range(1, KERNEL):
        same_doc = (shift_down(documents, offset, -2) == documents)[:, None]
        masked_grad = jnp.where(same_doc, d_mixed, 0.0)
        d_values = d_values + shift_up(masked_grad, offset, 0.0) * tap_weights[offset]
        tap_rows.append(jnp.sum(masked_grad * shift_down(values_pre, offset, 0.0), axis=0))
    conv_local = jnp.stack(tap_rows)
    d_query_key = jnp.stack([d_queries, d_keys], axis=1)
    delta_worth_opener = jnp.stack([d_values.astype(jnp.bfloat16), d_gates], axis=1)
    early_rows = sum_rows(
        normed,
        jnp.concatenate(
            [
                d_gates,
                d_values.astype(jnp.bfloat16),
                d_queries,
                d_keys,
            ],
            axis=1,
        ),
        2,
    )
    width = query_key.shape[2]
    value_gate_grad = jnp.stack(
        [early_rows[:, feature_share : 2 * feature_share], early_rows[:, :feature_share]], axis=1
    )
    query_key_grad = early_rows[:, 2 * feature_share :].reshape(-1, 2, width)
    d_normed_part = jnp.einsum(
        "tsf,dsf->td", d_query_key, query_key, preferred_element_type=jnp.float32
    )
    d_normed_part = d_normed_part + jnp.einsum(
        "tsf,dsf->td", delta_worth_opener, value_gate, preferred_element_type=jnp.float32
    )
    row_part = jnp.sum(d_normed_part * (unit_one * gain_one), axis=1)
    d_normed_own = sum_features(d_normed_part)
    row_sum = row_part
    for distance in (1, 2):
        row_sum = row_sum + swap_tensor(row_sum, distance)
    row_mean = row_sum[:, None] / model_width
    unit_one_own = own_columns(unit_one)
    input_grad = own_columns(d_hidden) + root_one * (
        d_normed_own * gains[0].astype(jnp.float32) - unit_one_own * row_mean
    )
    gain_one_grad = jnp.sum(d_normed_own * unit_one_own, axis=0)
    small = sum_dp(
        jnp.concatenate(
            [gain_one_grad[None], gain_two_grad[None], conv_local, jnp.zeros((2, feature_share))],
            axis=0,
        )
    )
    gains_grad = small[:2]
    conv_taps_grad = small[2:6]
    output_weight_grad = output_grad_rows.T
    down_weight_grad = down_grad_rows.T
    dp_index = lax.axis_index("dp")
    dp_count = lax.axis_size("dp")

    def own_rows(source, axis_dim):
        length = source.shape[axis_dim] // dp_count
        return lax.dynamic_slice_in_dim(source, dp_index * length, length, axis_dim)

    gains_change, gains_momentum, gains_average = advance(
        gains_grad, gains, gains_moment, gains_mean
    )
    query_key_change, query_key_momentum, query_key_average = advance(
        query_key_grad, own_rows(query_key, 0), query_key_moment, probe_lookup_smoothed
    )
    value_gate_change, value_gate_momentum, value_gate_average = advance(
        value_gate_grad, own_rows(value_gate, 0), value_gate_moment, value_gate_mean
    )
    conv_taps_change, conv_taps_momentum, conv_taps_average = advance(
        conv_taps_grad, conv_taps, conv_taps_moment, conv_taps_mean
    )
    output_weight_change, output_weight_momentum, output_weight_average = advance(
        output_weight_grad, own_rows(output_weight, 1), output_weight_moment, output_weight_mean
    )
    gate_up_change, gate_up_momentum, gate_up_average = advance(
        gate_up_grad, own_rows(gate_up, 0), gate_up_moment, gate_up_mean
    )
    down_weight_change, down_weight_momentum, down_weight_average = advance(
        down_weight_grad, own_rows(down_weight, 1), down_weight_moment, down_weight_mean
    )
    return (
        mixed,
        input_grad,
        gains_grad,
        query_key_grad,
        value_gate_grad,
        conv_taps_grad,
        output_weight_grad,
        gate_up_grad,
        down_weight_grad,
        gains_change,
        query_key_change,
        value_gate_change,
        conv_taps_change,
        output_weight_change,
        gate_up_change,
        down_weight_change,
        gains_momentum,
        query_key_momentum,
        value_gate_momentum,
        conv_taps_momentum,
        output_weight_momentum,
        gate_up_momentum,
        down_weight_momentum,
        gains_average,
        query_key_average,
        value_gate_average,
        conv_taps_average,
        output_weight_average,
        gate_up_average,
        down_weight_average,
    )


def solution(mesh):
    return jax.shard_map(
        local,
        mesh=mesh,
        in_specs=(
            P("dp", "tensor"),
            P("dp", "tensor"),
            P("dp"),
            P(None, "tensor"),
            P(None, None, "tensor"),
            P(None, None, "tensor"),
            P(None, "tensor"),
            P("tensor", None),
            P(None, None, "tensor"),
            P("tensor", None),
            P(None, "tensor"),
            P("dp", None, "tensor"),
            P("dp", None, "tensor"),
            P(None, "tensor"),
            P("tensor", "dp"),
            P("dp", None, "tensor"),
            P("tensor", "dp"),
            P(None, "tensor"),
            P("dp", None, "tensor"),
            P("dp", None, "tensor"),
            P(None, "tensor"),
            P("tensor", "dp"),
            P("dp", None, "tensor"),
            P("tensor", "dp"),
        ),
        out_specs=(
            P("dp", "tensor"),
            P("dp", "tensor"),
            P(None, "tensor"),
            P("dp", None, "tensor"),
            P("dp", None, "tensor"),
            P(None, "tensor"),
            P("tensor", "dp"),
            P("dp", None, "tensor"),
            P("tensor", "dp"),
            P(None, "tensor"),
            P("dp", None, "tensor"),
            P("dp", None, "tensor"),
            P(None, "tensor"),
            P("tensor", "dp"),
            P("dp", None, "tensor"),
            P("tensor", "dp"),
            P(None, "tensor"),
            P("dp", None, "tensor"),
            P("dp", None, "tensor"),
            P(None, "tensor"),
            P("tensor", "dp"),
            P("dp", None, "tensor"),
            P("tensor", "dp"),
            P(None, "tensor"),
            P("dp", None, "tensor"),
            P("dp", None, "tensor"),
            P(None, "tensor"),
            P("tensor", "dp"),
            P("dp", None, "tensor"),
            P("tensor", "dp"),
        ),
        check_vma=False,
    )
```

```python
import math

import jax
import jax.numpy as jnp
from jax import lax
from jax.experimental import pallas as pl
from jax.experimental.pallas import tpu as pltpu
from jax.sharding import PartitionSpec as P

H = 16
F = 16
KERNEL = 4
BLOCK = 256
EXTRA = 16


epsilon = 1e-06
momentum_decay = 0.9
learning_rate = 0.001
average_rate = 0.1

BF = jnp.bfloat16
F32 = jnp.float32
SCALE = 1.0 / math.sqrt(F)


def advance(grad, weight, moment, average):
    moment_new = momentum_decay * moment + (1.0 - momentum_decay) * grad
    change = -learning_rate * ((1.0 - momentum_decay) * grad + momentum_decay * moment_new)
    average_new = average + average_rate * (weight.astype(jnp.float32) + change - average)
    return (change, moment_new, average_new)


def shaped(*shape, dtype=F32):
    return jax.ShapeDtypeStruct(shape, dtype)


def whole():
    return pl.BlockSpec(memory_space=pltpu.VMEM)


def scalars():
    return pl.BlockSpec(memory_space=pltpu.SMEM)


def cost(flops, moved):
    return pl.CostEstimate(flops=int(flops), transcendentals=0, bytes_accessed=int(moved))


def dot(left, right, left_dim=1, right_dim=0):
    return lax.dot_general(
        left, right, (((left_dim,), (right_dim,)), ((), ())), preferred_element_type=F32
    )


def slope_of(argument, logistic):
    return logistic * (1.0 + argument * (1.0 - logistic))


def take(source, axis_dim, index):
    return lax.dynamic_index_in_dim(source, index, axis_dim, keepdims=False)


def own_bit(bit):
    return (lax.axis_index("dp") >> bit) & 1


def swap_dp(source, bit):
    count = lax.axis_size("dp")
    return lax.ppermute(source, "dp", [(k, k ^ (1 << bit)) for k in range(count)])


def swap_tensor(source, distance):
    count = lax.axis_size("tensor")
    return lax.ppermute(source, "tensor", [(k, k ^ distance) for k in range(count)])


def sum_dp(source):
    for bit in range(lax.axis_size("dp").bit_length() - 1):
        source = source + swap_dp(source, bit)
    return source


def gather_rows(source):
    count = lax.axis_size("tensor")
    own = lax.axis_index("tensor")
    pieces = [source] + [swap_tensor(source, distance) for distance in range(1, count)]
    out = jnp.zeros((count,) + source.shape, source.dtype)
    for distance, piece in enumerate(pieces):
        out = lax.dynamic_update_index_in_dim(out, piece, own ^ distance, 0)
    return out.reshape(count * source.shape[0], source.shape[1])


def norm_kernel(packed_ref, x_ref, turned_ref, normed_ref, root_ref, gain_ref, wide_ref):
    count, rows, tokens = packed_ref.shape
    share = rows - EXTRA
    width = count * share
    total = jnp.zeros((1, tokens), F32)
    for k in range(count):
        block = packed_ref[k, :share, :].astype(F32)
        total = total + jnp.sum(block * block, axis=0, keepdims=True)
    root = lax.rsqrt(total / width + epsilon)
    root_ref[...] = jnp.broadcast_to(root, root_ref.shape)
    for k in range(count):
        first = k * share
        turned = packed_ref[k, share:, :].astype(F32).T
        at = 0
        for piece in range(-(-share // tokens)):
            length = min(tokens, share - at)
            gain_ref[first + at : first + at + length, :] = turned[
                :length, 2 * piece : 2 * piece + 2
            ]
            at += length
        block = packed_ref[k, :share, :]
        x_ref[first : first + share, :] = block
        wide_ref[first : first + share, :] = (
            block.astype(F32) * root * gain_ref[first : first + share, 0:1]
        )
    for start in range(0, width, 256):
        piece = wide_ref[start : start + 256, :]
        turned_ref[start : start + 256, :] = piece.astype(BF)
        normed_ref[:, start : start + 256] = piece.T.astype(BF)


def send_blocks(own, wide_ref, keep_ref, send_refs):
    share = keep_ref.shape[0]
    keep_ref[...] = wide_ref[pl.ds(pl.multiple_of(own * share, share), share), :]
    for k, send_ref in enumerate(send_refs):
        at = pl.multiple_of((own ^ (k + 1)) * share, share)
        send_ref[:share, :] = wide_ref[pl.ds(at, share), :].astype(BF)


def allowed_pairs(column_ref, row_ref):
    tokens = column_ref.shape[0]
    row_index = lax.broadcasted_iota(jnp.int32, (tokens, tokens), 0)
    column_index = lax.broadcasted_iota(jnp.int32, (tokens, tokens), 1)
    return (column_ref[...] == row_ref[...]) & (column_index <= row_index)


def weigh(queries, keys, allowed):
    scores = dot(queries, keys, 1, 1) * SCALE
    weights = jnp.where(allowed, 1.0 + scores + 0.5 * scores * scores, 0.0)
    return scores, weights, jnp.sum(weights, axis=1, keepdims=True)


def mix_kernel(
    own_ref, q_ref, k_ref, v_ref, g_ref, taps_ref, mask_ref, column_ref, row_ref, out_w_ref,
    mixed_ref, attended_ref, gated_ref, keep_ref, *rest,
):
    send_refs, (shift_ref, wide_ref) = rest[:-2], rest[-2:]
    tokens, share = v_ref.shape
    heads = q_ref.shape[1] // F
    size = share // heads
    taps = taps_ref[...].astype(F32)
    values = v_ref[...]
    shift_ref[0:8, :] = jnp.zeros((8, share), F32)
    shift_ref[8 : 8 + tokens, :] = values
    summed = values * taps[0:1]
    for j in range(1, KERNEL):
        summed = summed + mask_ref[:, j : j + 1] * (
            shift_ref[8 - j : 8 - j + tokens, :] * taps[j : j + 1]
        )
    mixed_ref[...] = summed.astype(BF)
    allowed = allowed_pairs(column_ref, row_ref)
    for h in range(heads):
        feats = slice(h * F, (h + 1) * F)
        vals = slice(h * size, (h + 1) * size)
        _, weights, totals = weigh(q_ref[:, feats], k_ref[:, feats], allowed)
        attended_ref[:, vals] = dot((weights / totals).astype(BF), mixed_ref[:, vals])
    gates = g_ref[...]
    gated = (attended_ref[...] * (gates * jax.nn.sigmoid(gates))).astype(BF)
    gated_ref[...] = gated
    for start in range(0, wide_ref.shape[0], 256):
        wide_ref[start : start + 256, :] = dot(gated, out_w_ref[:, start : start + 256]).T
    send_blocks(own_ref[0], wide_ref, keep_ref, send_refs)


def ffn_kernel(
    own_ref, hidden_ref, gain_ref, cot_ref, gate_ref, up_ref, down_ref,
    turned_ref, root_ref, act_ref, d_gate_ref, d_up_ref, keep_ref, *rest,
):
    send_refs, (normed_ref, wide_ref) = rest[:-2], rest[-2:]
    width, tokens = hidden_ref.shape
    step = pl.program_id(0)

    @pl.when(step == 0)
    def _():
        total = jnp.zeros((1, tokens), F32)
        for start in range(0, width, 256):
            block = hidden_ref[start : start + 256, :].astype(F32)
            total = total + jnp.sum(block * block, axis=0, keepdims=True)
        root = lax.rsqrt(total / width + epsilon)
        root_ref[...] = jnp.broadcast_to(root, root_ref.shape)
        for start in range(0, width, 256):
            piece = (
                hidden_ref[start : start + 256, :].astype(F32)
                * root
                * gain_ref[start : start + 256, 1:2]
            )
            turned_ref[start : start + 256, :] = piece.astype(BF)
            normed_ref[:, start : start + 256] = piece.T.astype(BF)
            wide_ref[start : start + 256, :] = jnp.zeros((256, tokens), F32)

    normed = normed_ref[...]
    gate = dot(normed, gate_ref[...])
    up = dot(normed, up_ref[...])
    d_act = dot(down_ref[...], cot_ref[...]).T
    logistic = jax.nn.sigmoid(gate)
    silu = gate * logistic
    act_ref[...] = (silu * up).astype(BF)
    d_gate_ref[...] = (d_act * up * slope_of(gate, logistic)).astype(BF)
    d_up_ref[...] = (d_act * silu).astype(BF)
    for start in range(0, width, 256):
        rows = slice(start, start + 256)
        wide_ref[rows, :] = (
            wide_ref[rows, :]
            + dot(gate_ref[rows, :], d_gate_ref[...], 1, 1)
            + dot(up_ref[rows, :], d_up_ref[...], 1, 1)
        )

    @pl.when(step == pl.num_programs(0) - 1)
    def _():
        send_blocks(own_ref[0], wide_ref, keep_ref, send_refs)


def feed_kernel(own_ref, act_ref, down_ref, keep_ref, *rest):
    send_refs, (wide_ref,) = rest[:-1], rest[-1:]
    for start in range(0, wide_ref.shape[0], 256):
        wide_ref[start : start + 256, :] = dot(act_ref[...], down_ref[:, start : start + 256]).T
    send_blocks(own_ref[0], wide_ref, keep_ref, send_refs)


def add_kernel(count, *refs):
    keep_ref, arrived = refs[0], refs[1:count]
    out_ref, rounded_ref = refs[-2:]
    total = keep_ref[...]
    for ref in arrived:
        total = total + ref[...].astype(F32)
    out_ref[...] = total
    rounded_ref[...] = total.astype(BF)


def back_kernel(
    own_ref, d_normed_ref, hidden_ref, root_two_ref, gain_ref, cot_ref, x_ref, root_one_ref,
    out_w_ref, q_ref, k_ref, v_ref, g_ref, attended_ref, mixed_ref, taps_ref, mask_ref,
    column_ref, row_ref, wq_ref, wk_ref, wv_ref, wg_ref,
    d_hidden_ref, branch_ref, delta_ref, small_ref, keep_ref, line_ref, *rest,
):
    send_refs, (wide_ref, d_branch_ref, shift_ref, d_mixed_ref) = rest[:-4], rest[-4:]
    width, tokens = hidden_ref.shape
    share = v_ref.shape[1]
    heads = q_ref.shape[1] // F
    size = share // heads
    own = own_ref[0]
    root_two = root_two_ref[0:1, :]
    total = jnp.zeros((1, tokens), F32)
    for start in range(0, width, 256):
        rows = slice(start, start + 256)
        unit = hidden_ref[rows, :].astype(F32) * root_two
        scaled = d_normed_ref[rows, :].astype(F32) * gain_ref[rows, 1:2]
        total = total + jnp.sum(scaled * unit, axis=0, keepdims=True)
    mean = total / width
    for start in range(0, width, 256):
        rows = slice(start, start + 256)
        unit = hidden_ref[rows, :].astype(F32) * root_two
        scaled = d_normed_ref[rows, :].astype(F32) * gain_ref[rows, 1:2]
        piece = cot_ref[rows, :].astype(F32) + root_two * (scaled - unit * mean)
        wide_ref[rows, :] = piece
        branch_ref[rows, :] = piece.astype(BF)
        d_branch_ref[:, rows] = piece.T.astype(BF)
    d_hidden_ref[...] = wide_ref[pl.ds(pl.multiple_of(own * share, share), share), :]
    d_gated = dot(d_branch_ref[...], out_w_ref[...], 1, 1)
    gates = g_ref[...]
    logistic = jax.nn.sigmoid(gates)
    d_attended = (d_gated * (gates * logistic)).astype(BF)
    delta_ref[:, :share] = (d_gated * attended_ref[...] * slope_of(gates, logistic)).astype(BF)
    shift_ref[8 : 8 + tokens, :] = d_attended.astype(F32)
    allowed = allowed_pairs(column_ref, row_ref)
    first = 2 * share
    for h in range(heads):
        feats = slice(h * F, (h + 1) * F)
        vals = slice(h * size, (h + 1) * size)
        queries, keys = q_ref[:, feats], k_ref[:, feats]
        scores, weights, totals = weigh(queries, keys, allowed)
        probs = weights / totals
        d_att = shift_ref[8 : 8 + tokens, vals].astype(BF)
        d_mixed_ref[:, vals] = dot(probs.T.astype(BF), d_att)
        d_probs = dot(d_att, mixed_ref[:, vals], 1, 1)
        d_weights = (d_probs - jnp.sum(d_probs * probs, axis=1, keepdims=True)) / totals
        d_scores = jnp.where(allowed, d_weights * (1.0 + scores), 0.0)
        d_q = dot(d_scores.astype(BF), keys) * SCALE
        d_k = dot(d_scores.T.astype(BF), queries) * SCALE
        delta_ref[:, first + h * F : first + (h + 1) * F] = d_q.astype(BF)
        at = first + heads * F
        delta_ref[:, at + h * F : at + (h + 1) * F] = d_k.astype(BF)
    taps = taps_ref[...].astype(F32)
    d_mixed = d_mixed_ref[...]
    values = v_ref[...]
    small_ref[...] = jnp.zeros(small_ref.shape, F32)
    small_ref[0:1, :] = jnp.sum(d_mixed * values, axis=0, keepdims=True)
    shift_ref[0:8, :] = jnp.zeros((8, share), F32)
    shift_ref[8 : 8 + tokens, :] = values
    for j in range(1, KERNEL):
        masked = mask_ref[:, j : j + 1] * d_mixed
        small_ref[j : j + 1, :] = jnp.sum(
            masked * shift_ref[8 - j : 8 - j + tokens, :], axis=0, keepdims=True
        )
    d_values = d_mixed * taps[0:1]
    shift_ref[8 + tokens : 16 + tokens, :] = jnp.zeros((8, share), F32)
    for j in range(1, KERNEL):
        shift_ref[8 : 8 + tokens, :] = mask_ref[:, j : j + 1] * d_mixed
        d_values = d_values + shift_ref[8 + j : 8 + j + tokens, :] * taps[j : j + 1]
    delta_ref[:, share : 2 * share] = d_values.astype(BF)
    d_gates = delta_ref[:, :share]
    d_values = delta_ref[:, share : 2 * share]
    d_queries = delta_ref[:, first : first + heads * F]
    d_keys = delta_ref[:, first + heads * F : first + 2 * heads * F]
    root_one = root_one_ref[0:1, :]
    line = jnp.zeros((1, tokens), F32)
    for start in range(0, width, 256):
        rows = slice(start, start + 256)
        piece = (
            dot(wq_ref[rows, :], d_queries, 1, 1)
            + dot(wk_ref[rows, :], d_keys, 1, 1)
            + dot(wv_ref[rows, :], d_values, 1, 1)
            + dot(wg_ref[rows, :], d_gates, 1, 1)
        )
        wide_ref[rows, :] = piece
        unit = x_ref[rows, :].astype(F32) * root_one
        line = line + jnp.sum(piece * (unit * gain_ref[rows, 0:1]), axis=0, keepdims=True)
    line_ref[...] = jnp.broadcast_to(line, line_ref.shape)
    send_blocks(own, wide_ref, keep_ref, send_refs)
    high = line.astype(BF)
    low = (line - high.astype(F32)).astype(BF)
    index = lax.broadcasted_iota(jnp.int32, (EXTRA, tokens), 0)
    extra = jnp.where(
        index == 0,
        jnp.broadcast_to(high.astype(F32), (EXTRA, tokens)),
        jnp.where(index == 1, jnp.broadcast_to(low.astype(F32), (EXTRA, tokens)), 0.0),
    ).astype(BF)
    for send_ref in send_refs:
        send_ref[share:, :] = extra


def first_kernel(plans, n_left, n_right, where_ref, *refs):
    lefts, rights = refs[:n_left], refs[n_left : n_left + n_right]
    outs = refs[n_left + n_right :]
    for plan, out_ref in zip(plans, outs):
        at = 0
        for left, right, start, length in plan:
            out_ref[0, :, at : at + length] = dot(
                lefts[left][0, 0], rights[right][:, start : start + length]
            ).astype(BF)
            at += length


def second_kernel(plans, n_left, n_right, where_ref, *refs):
    count = len(plans)
    lefts = refs[: n_left * count]
    rights = refs[n_left * count : n_left * count + n_right]
    arrived = refs[n_left * count + n_right :][:count]
    outs = refs[n_left * count + n_right + count :]
    phase = pl.program_id(0)
    for p, plan in enumerate(plans):

        def value(left, right, start, length, at, p=p):
            return (
                dot(lefts[p * n_left + left][0, 0], rights[right][:, start : start + length])
                + arrived[p][0, :, at : at + length].astype(F32)
            )

        @pl.when(phase == 0)
        def _(p=p, plan=plan, value=value):
            at = 0
            for left, right, start, length in plan:
                outs[2 * p][0, :, at : at + length] = value(left, right, start, length, at).astype(BF)
                at += length

        @pl.when(phase == 1)
        def _(p=p, plan=plan, value=value):
            at = 0
            for left, right, start, length in plan:
                outs[2 * p + 1][0, :, at : at + length] = value(left, right, start, length, at)
                at += length


def sum_rows_first(lefts, rights, plans, name):
    count = lax.axis_size("dp")
    width, tokens = lefts[0].shape
    rows = width // count
    half = count // 2
    views = [left.reshape(half, 2, rows, tokens) for left in lefts]
    where = jnp.stack([1 - own_bit(0)]).astype(jnp.int32)
    sizes = [sum(piece[3] for piece in plan) for plan in plans]
    grid_spec = pltpu.PrefetchScalarGridSpec(
        num_scalar_prefetch=1,
        grid=(half,),
        in_specs=[
            pl.BlockSpec((1, 1, rows, tokens), lambda g, at: (g, at[0], 0, 0)) for _ in views
        ]
        + [pl.BlockSpec(right.shape, lambda g, at: (0, 0)) for right in rights],
        out_specs=[pl.BlockSpec((1, rows, size), lambda g, at: (g, 0, 0)) for size in sizes],
    )
    flops = 2 * half * rows * tokens * sum(sizes)
    sends = pl.pallas_call(
        lambda *refs: first_kernel(plans, len(views), len(rights), *refs),
        out_shape=[shaped(half, rows, size, dtype=BF) for size in sizes],
        grid_spec=grid_spec,
        cost_estimate=cost(flops, 2 * half * rows * sum(sizes)),
        name=name,
    )(where, *views, *rights)
    return [swap_dp(send, 0) for send in sends]


def path_orders(bits):
    return [list(range(1, bits)), list(reversed(range(1, bits)))]


def sum_rows_second(lefts, rights, plans, arrived, name):
    count = lax.axis_size("dp")
    bits = count.bit_length() - 1
    width, tokens = lefts[0].shape
    rows = width // count
    half, quarter = count // 2, count // 4
    views = [left.reshape(half, 2, rows, tokens) for left in lefts]
    orders = path_orders(bits)
    cuts = [order[0] - 1 for order in orders]
    where = jnp.stack([own_bit(0)] + [own_bit(order[0]) for order in orders]).astype(jnp.int32)
    sizes = [sum(piece[3] for piece in plan) for plan in plans]

    def block_of(p, phase, q, at):
        cut = cuts[p]
        bit = jnp.where(phase == 0, 1 - at[1 + p], at[1 + p])
        return ((q >> cut) << (cut + 1)) | (bit << cut) | (q & ((1 << cut) - 1))

    in_specs = []
    operands = []
    for p in range(len(plans)):
        for view in views:
            in_specs.append(
                pl.BlockSpec(
                    (1, 1, rows, tokens),
                    lambda phase, q, at, p=p: (block_of(p, phase, q, at), at[0], 0, 0),
                )
            )
            operands.append(view)
    for right in rights:
        in_specs.append(pl.BlockSpec(right.shape, lambda phase, q, at: (0, 0)))
        operands.append(right)
    for p, piece in enumerate(arrived):
        in_specs.append(
            pl.BlockSpec(
                (1, rows, sizes[p]), lambda phase, q, at, p=p: (block_of(p, phase, q, at), 0, 0)
            )
        )
        operands.append(piece)
    out_specs, out_shape = [], []
    for size in sizes:
        out_specs.append(
            pl.BlockSpec(
                (1, rows, size),
                lambda phase, q, at: (jnp.where(phase == 0, q, quarter - 1), 0, 0),
            )
        )
        out_shape.append(shaped(quarter, rows, size, dtype=BF))
        out_specs.append(
            pl.BlockSpec(
                (1, rows, size), lambda phase, q, at: (jnp.where(phase == 1, q, 0), 0, 0)
            )
        )
        out_shape.append(shaped(quarter, rows, size))
    outs = pl.pallas_call(
        lambda *refs: second_kernel(plans, len(views), len(rights), *refs),
        out_shape=out_shape,
        grid_spec=pltpu.PrefetchScalarGridSpec(
            num_scalar_prefetch=1, grid=(2, quarter), in_specs=in_specs, out_specs=out_specs
        ),
        cost_estimate=cost(2 * half * rows * tokens * sum(sizes), 5 * half * rows * sum(sizes)),
        name=name,
    )(where, *operands)
    return [(outs[2 * p], outs[2 * p + 1]) for p in range(len(plans))]


def sum_rows_third(halves):
    bits = lax.axis_size("dp").bit_length() - 1
    results = []
    for order, (send, keep) in zip(path_orders(bits), halves):
        total = keep + swap_dp(send, order[0]).astype(F32)
        remaining = [bit for bit in reversed(range(1, bits)) if bit != order[0]]
        total = total.reshape((2,) * len(remaining) + total.shape[1:])
        for bit in order[1:]:
            at = remaining.index(bit)
            received = swap_dp(take(total, at, 1 - own_bit(bit)).astype(BF), bit)
            total = take(total, at, own_bit(bit)) + received.astype(F32)
            remaining.pop(at)
        results.append(total)
    return results


def local(
    inputs,
    cotangent,
    documents,
    gains,
    query_key,
    value_gate,
    conv_taps,
    output_weight,
    gate_up,
    down_weight,
    gains_moment,
    query_key_moment,
    value_gate_moment,
    conv_taps_moment,
    output_weight_moment,
    gate_up_moment,
    down_weight_moment,
    gains_mean,
    probe_lookup_smoothed,
    value_gate_mean,
    conv_taps_mean,
    output_weight_mean,
    gate_up_mean,
    down_weight_mean,
):
    tokens, share = inputs.shape
    groups = lax.axis_size("tensor")
    width = share * groups
    heads = H // groups
    key_width = heads * F
    hidden_units = down_weight.shape[0]
    own = lax.axis_index("tensor")
    own_index = own.astype(jnp.int32).reshape(1)

    inputs_turned = inputs.T
    pieces = -(-share // tokens)
    gain_lines = jnp.pad(gains, ((0, 0), (0, pieces * tokens - share)))
    gain_lines = gain_lines.reshape(2, pieces, tokens).transpose(1, 0, 2).reshape(-1, tokens)
    packed = jnp.concatenate(
        [inputs_turned, jnp.pad(gain_lines, ((0, EXTRA - 2 * pieces), (0, 0)))], axis=0
    )
    packed_whole = lax.all_gather(packed, "tensor")
    documents_column = documents[:, None]
    documents_row = documents[None, :]
    masks = [jnp.ones((tokens,), F32)]
    for offset in range(1, KERNEL):
        earlier = jnp.pad(documents, (offset, 0), constant_values=-2)[:tokens]
        masks.append((earlier == documents).astype(F32))
    masks = jnp.stack(masks, axis=1)
    masked = jnp.where(documents_column >= 0, cotangent, jnp.zeros_like(cotangent)).T
    masked, packed_whole = lax.optimization_barrier((masked, packed_whole))

    x_turned, normed_turned, normed, root_one, gain_columns = pl.pallas_call(
        norm_kernel,
        out_shape=[
            shaped(width, tokens, dtype=BF),
            shaped(width, tokens, dtype=BF),
            shaped(tokens, width, dtype=BF),
            shaped(8, tokens),
            shaped(width, 2),
        ],
        scratch_shapes=[pltpu.VMEM((width, tokens), F32)],
        cost_estimate=cost(10 * width * tokens, 8 * width * tokens),
        name="norm_one",
    )(packed_whole)
    cot_turned = gather_rows(masked)
    projected = jnp.einsum("td,dsf->tsf", normed, query_key, preferred_element_type=F32).astype(BF)
    mixing = jnp.einsum("td,dsf->tsf", normed, value_gate, preferred_element_type=F32)
    queries, keys = projected[:, 0], projected[:, 1]
    values_pre, gates = mixing[:, 0], mixing[:, 1]

    def sends(extra=0):
        return [shaped(share + extra, tokens, dtype=BF) for _ in range(groups - 1)]

    vmem = whole()
    mixed_values, attended, gated, branch_keep, *branch_sends = pl.pallas_call(
        mix_kernel,
        out_shape=[
            shaped(tokens, share, dtype=BF),
            shaped(tokens, share),
            shaped(tokens, share, dtype=BF),
            shaped(share, tokens),
        ]
        + sends(),
        in_specs=[scalars()] + [vmem] * 9,
        scratch_shapes=[pltpu.VMEM((tokens + 16, share), F32), pltpu.VMEM((width, tokens), F32)],
        cost_estimate=cost(2 * tokens * share * width, 4 * share * width),
        name="mix_forward",
    )(
        own_index, queries, keys, values_pre, gates, conv_taps, masks, documents_column,
        documents_row, output_weight,
    )
    arrived = [swap_tensor(send, k + 1) for k, send in enumerate(branch_sends)]
    gate_weight, up_weight = gate_up[:, 0], gate_up[:, 1]
    hidden_own = inputs_turned.astype(F32) + branch_keep
    for piece in arrived:
        hidden_own = hidden_own + piece.astype(F32)
    hidden = lax.all_gather(hidden_own.astype(BF), "tensor", axis=0, tiled=True)

    tile = 256
    normed_two_turned, root_two, activation, d_gate, d_up, keep_two, *sends_two = pl.pallas_call(
        ffn_kernel,
        out_shape=[
            shaped(width, tokens, dtype=BF),
            shaped(8, tokens),
            shaped(tokens, hidden_units, dtype=BF),
            shaped(tokens, hidden_units, dtype=BF),
            shaped(tokens, hidden_units, dtype=BF),
            shaped(share, tokens),
        ]
        + sends(),
        grid=(hidden_units // tile,),
        in_specs=[
            scalars(),
            pl.BlockSpec((width, tokens), lambda f: (0, 0)),
            pl.BlockSpec((width, 2), lambda f: (0, 0)),
            pl.BlockSpec((width, tokens), lambda f: (0, 0)),
            pl.BlockSpec((width, tile), lambda f: (0, f)),
            pl.BlockSpec((width, tile), lambda f: (0, f)),
            pl.BlockSpec((tile, width), lambda f: (f, 0)),
        ],
        out_specs=[
            pl.BlockSpec((width, tokens), lambda f: (0, 0)),
            pl.BlockSpec((8, tokens), lambda f: (0, 0)),
            pl.BlockSpec((tokens, tile), lambda f: (0, f)),
            pl.BlockSpec((tokens, tile), lambda f: (0, f)),
            pl.BlockSpec((tokens, tile), lambda f: (0, f)),
            pl.BlockSpec((share, tokens), lambda f: (0, 0)),
        ]
        + [pl.BlockSpec((share, tokens), lambda f: (0, 0)) for _ in range(groups - 1)],
        scratch_shapes=[pltpu.VMEM((tokens, width), BF), pltpu.VMEM((width, tokens), F32)],
        cost_estimate=cost(10 * tokens * width * hidden_units, 6 * width * hidden_units),
        name="ffn",
    )(own_index, hidden, gain_columns, cot_turned, gate_weight, up_weight, down_weight)
    arrived_two = [swap_tensor(send, k + 1) for k, send in enumerate(sends_two)]

    middle = hidden_units // 2
    ffn_plans = (
        ((0, 0, 0, hidden_units), (0, 1, 0, middle)),
        ((0, 1, middle, hidden_units - middle), (1, 2, 0, hidden_units)),
    )
    ffn_lefts = (normed_two_turned, cot_turned)
    ffn_rights = (d_gate, d_up, activation)
    ffn_arrived = sum_rows_first(ffn_lefts, ffn_rights, ffn_plans, "ffn_grad_first")
    ffn_halves = sum_rows_second(ffn_lefts, ffn_rights, ffn_plans, ffn_arrived, "ffn_grad_second")

    d_normed_two_own, d_normed_two_rounded = pl.pallas_call(
        lambda *refs: add_kernel(groups, *refs),
        out_shape=[shaped(share, tokens), shaped(share, tokens, dtype=BF)],
        in_specs=[vmem] * groups + [pl.BlockSpec(memory_space=pl.ANY)] * 2,
        cost_estimate=cost(4 * share * tokens, 14 * share * tokens),
        name="add_two",
    )(keep_two, *arrived_two, ffn_halves[0][0], ffn_halves[1][0])
    d_normed_two = lax.all_gather(d_normed_two_rounded, "tensor", axis=0, tiled=True)
    ffn_rows = sum_rows_third(ffn_halves)
    wq, wk = query_key[:, 0], query_key[:, 1]
    wv, wg = value_gate[:, 0], value_gate[:, 1]
    feed_keep, *feed_sends = pl.pallas_call(
        feed_kernel,
        out_shape=[shaped(share, tokens)] + sends(),
        in_specs=[scalars(), vmem, vmem],
        scratch_shapes=[pltpu.VMEM((width, tokens), F32)],
        cost_estimate=cost(2 * tokens * width * hidden_units, 2 * width * hidden_units),
        name="feed",
    )(own_index, activation, down_weight)

    d_hidden_own, d_branch_turned, delta, taps_part, keep_one, line_one, *sends_one = (
        pl.pallas_call(
            back_kernel,
            out_shape=[
                shaped(share, tokens),
                shaped(width, tokens, dtype=BF),
                shaped(tokens, 2 * (share + key_width), dtype=BF),
                shaped(8, share),
                shaped(share, tokens),
                shaped(8, tokens),
            ]
            + sends(EXTRA),
            in_specs=[scalars()] + [vmem] * 22,
            scratch_shapes=[
                pltpu.VMEM((width, tokens), F32),
                pltpu.VMEM((tokens, width), BF),
                pltpu.VMEM((tokens + 16, share), F32),
                pltpu.VMEM((tokens, share), F32),
            ],
            cost_estimate=cost(8 * tokens * width * share, 20 * width * share),
            name="mix_backward",
        )(
            own_index, d_normed_two, hidden, root_two, gain_columns, cot_turned, x_turned,
            root_one, output_weight, queries, keys, values_pre, gates, attended, mixed_values,
            conv_taps, masks, documents_column, documents_row, wq, wk, wv, wg,
        )
    )
    arrived_one = [swap_tensor(send, k + 1) for k, send in enumerate(sends_one)]
    all_columns = 2 * (share + key_width)
    cut = (all_columns * 3 // 4) // 128 * 128
    mix_plans = (
        ((0, 0, cut, all_columns - cut), (1, 1, 0, share)),
        ((0, 0, 0, cut),),
    )
    mix_lefts = (normed_turned, d_branch_turned)
    mix_rights = (delta, gated)
    mix_arrived = sum_rows_first(mix_lefts, mix_rights, mix_plans, "mix_grad_first")
    mix_halves = sum_rows_second(mix_lefts, mix_rights, mix_plans, mix_arrived, "mix_grad_second")
    mix_rows = sum_rows_third(mix_halves)

    feed_own = feed_keep
    for k, send in enumerate(feed_sends):
        feed_own = feed_own + swap_tensor(send, k + 1).astype(F32)
    mixed = (hidden_own + feed_own).astype(BF).T

    def own_rows_of(source):
        return lax.dynamic_slice_in_dim(source, own * share, share, 0)

    gain_own = gains.astype(F32).T
    root_one_line, root_two_line = root_one[0:1], root_two[0:1]
    unit_two_own = own_rows_of(hidden).astype(F32) * root_two_line
    gain_two_grad = jnp.sum(d_normed_two_own * unit_two_own, axis=1)
    d_normed_own, line = keep_one, line_one[0:1]
    for piece in arrived_one:
        d_normed_own = d_normed_own + piece[:share].astype(F32)
        line = line + (piece[share : share + 1].astype(F32) + piece[share + 1 : share + 2].astype(F32))
    unit_one_own = inputs_turned.astype(F32) * root_one_line
    input_grad = (
        d_hidden_own
        + root_one_line * (d_normed_own * gain_own[:, 0:1] - unit_one_own * (line / width))
    ).T
    gain_one_grad = jnp.sum(d_normed_own * unit_one_own, axis=1)
    small = sum_dp(
        jnp.concatenate(
            [gain_one_grad[None], gain_two_grad[None], taps_part[:KERNEL], jnp.zeros((2, share))],
            axis=0,
        )
    )
    gains_grad = small[:2]
    conv_taps_grad = small[2 : 2 + KERNEL]
    ffn_a, ffn_b = ffn_rows
    rest = hidden_units - middle
    gate_up_grad = jnp.stack(
        [
            ffn_a[:, :hidden_units],
            jnp.concatenate([ffn_a[:, hidden_units:], ffn_b[:, :rest]], axis=1),
        ],
        axis=1,
    )
    down_weight_grad = ffn_b[:, rest:].T
    mix_a, mix_b = mix_rows
    columns = jnp.concatenate([mix_b, mix_a[:, : all_columns - cut]], axis=1)
    value_gate_grad = jnp.stack([columns[:, share : 2 * share], columns[:, :share]], axis=1)
    query_key_grad = columns[:, 2 * share :].reshape(-1, 2, key_width)
    output_weight_grad = mix_a[:, all_columns - cut :].T
    (
        gate_up_grad, down_weight_grad, value_gate_grad, query_key_grad, output_weight_grad,
    ) = [
        lax.optimization_barrier(grad)
        for grad in (
            gate_up_grad, down_weight_grad, value_gate_grad, query_key_grad, output_weight_grad,
        )
    ]
    dp_index = lax.axis_index("dp")
    dp_count = lax.axis_size("dp")

    def own_rows(source, axis_dim):
        length = source.shape[axis_dim] // dp_count
        return lax.dynamic_slice_in_dim(source, dp_index * length, length, axis_dim)

    gains_change, gains_momentum, gains_average = advance(
        gains_grad, gains, gains_moment, gains_mean
    )
    query_key_change, query_key_momentum, query_key_average = advance(
        query_key_grad, own_rows(query_key, 0), query_key_moment, probe_lookup_smoothed
    )
    value_gate_change, value_gate_momentum, value_gate_average = advance(
        value_gate_grad, own_rows(value_gate, 0), value_gate_moment, value_gate_mean
    )
    conv_taps_change, conv_taps_momentum, conv_taps_average = advance(
        conv_taps_grad, conv_taps, conv_taps_moment, conv_taps_mean
    )
    output_weight_change, output_weight_momentum, output_weight_average = advance(
        output_weight_grad, own_rows(output_weight, 1), output_weight_moment, output_weight_mean
    )
    gate_up_change, gate_up_momentum, gate_up_average = advance(
        gate_up_grad, own_rows(gate_up, 0), gate_up_moment, gate_up_mean
    )
    down_weight_change, down_weight_momentum, down_weight_average = advance(
        down_weight_grad, own_rows(down_weight, 1), down_weight_moment, down_weight_mean
    )
    return (
        mixed,
        input_grad,
        gains_grad,
        query_key_grad,
        value_gate_grad,
        conv_taps_grad,
        output_weight_grad,
        gate_up_grad,
        down_weight_grad,
        gains_change,
        query_key_change,
        value_gate_change,
        conv_taps_change,
        output_weight_change,
        gate_up_change,
        down_weight_change,
        gains_momentum,
        query_key_momentum,
        value_gate_momentum,
        conv_taps_momentum,
        output_weight_momentum,
        gate_up_momentum,
        down_weight_momentum,
        gains_average,
        query_key_average,
        value_gate_average,
        conv_taps_average,
        output_weight_average,
        gate_up_average,
        down_weight_average,
    )


def solution(mesh):
    return jax.shard_map(
        local,
        mesh=mesh,
        in_specs=(
            P("dp", "tensor"),
            P("dp", "tensor"),
            P("dp"),
            P(None, "tensor"),
            P(None, None, "tensor"),
            P(None, None, "tensor"),
            P(None, "tensor"),
            P("tensor", None),
            P(None, None, "tensor"),
            P("tensor", None),
            P(None, "tensor"),
            P("dp", None, "tensor"),
            P("dp", None, "tensor"),
            P(None, "tensor"),
            P("tensor", "dp"),
            P("dp", None, "tensor"),
            P("tensor", "dp"),
            P(None, "tensor"),
            P("dp", None, "tensor"),
            P("dp", None, "tensor"),
            P(None, "tensor"),
            P("tensor", "dp"),
            P("dp", None, "tensor"),
            P("tensor", "dp"),
        ),
        out_specs=(
            P("dp", "tensor"),
            P("dp", "tensor"),
            P(None, "tensor"),
            P("dp", None, "tensor"),
            P("dp", None, "tensor"),
            P(None, "tensor"),
            P("tensor", "dp"),
            P("dp", None, "tensor"),
            P("tensor", "dp"),
            P(None, "tensor"),
            P("dp", None, "tensor"),
            P("dp", None, "tensor"),
            P(None, "tensor"),
            P("tensor", "dp"),
            P("dp", None, "tensor"),
            P("tensor", "dp"),
            P(None, "tensor"),
            P("dp", None, "tensor"),
            P("dp", None, "tensor"),
            P(None, "tensor"),
            P("tensor", "dp"),
            P("dp", None, "tensor"),
            P("tensor", "dp"),
            P(None, "tensor"),
            P("dp", None, "tensor"),
            P("dp", None, "tensor"),
            P(None, "tensor"),
            P("tensor", "dp"),
            P("dp", None, "tensor"),
            P("tensor", "dp"),
        ),
        check_vma=False,
    )
```

```python
import math

import jax
import jax.numpy as jnp
from jax import lax
from jax.experimental import pallas as pl
from jax.experimental.pallas import tpu as pltpu
from jax.experimental.layout import Layout, with_layout_constraint
from jax.sharding import PartitionSpec as P

H = 16
F = 16
KERNEL = 4
EXTRA = 16


DP = "dp"
TENSOR = "tensor"

epsilon = 1e-06
momentum_decay = 0.9
learning_rate = 0.001
average_rate = 0.1

BF = jnp.bfloat16
F32 = jnp.float32
SCALE = 1.0 / math.sqrt(F)


def advance(grad, weight, moment, average):
    moment_new = momentum_decay * moment + (1.0 - momentum_decay) * grad
    change = -learning_rate * ((1.0 - momentum_decay) * grad + momentum_decay * moment_new)
    average_new = average + average_rate * (weight.astype(jnp.float32) + change - average)
    return (change, moment_new, average_new)


def shaped(*shape, dtype=F32):
    return jax.ShapeDtypeStruct(shape, dtype)


def whole():
    return pl.BlockSpec(memory_space=pltpu.VMEM)


def scalars():
    return pl.BlockSpec(memory_space=pltpu.SMEM)


def cost(flops, moved):
    return pl.CostEstimate(flops=int(flops), transcendentals=0, bytes_accessed=int(moved))


def dot(left, right, left_dim=1, right_dim=0):
    return lax.dot_general(
        left, right, (((left_dim,), (right_dim,)), ((), ())), preferred_element_type=F32
    )


def slope_of(argument, logistic):
    return logistic * (1.0 + argument * (1.0 - logistic))


def own_bit(bit):
    return (lax.axis_index(DP) >> bit) & 1


def swap_dp(source, bit):
    count = lax.axis_size(DP)
    return lax.ppermute(source, DP, [(k, k ^ (1 << bit)) for k in range(count)])


def swap_tensor(source, distance):
    count = lax.axis_size(TENSOR)
    return lax.ppermute(source, TENSOR, [(k, k ^ distance) for k in range(count)])


def sum_dp(source):
    for bit in range(lax.axis_size(DP).bit_length() - 1):
        source = source + swap_dp(source, bit)
    return source


def place_rows(own, whole_ref, pieces):
    share = pieces[0].shape[0]
    for k, piece in enumerate(pieces):
        at = pl.multiple_of((own ^ k) * share, share)
        whole_ref[pl.ds(at, share), :] = piece[...]


def send_blocks(own, wide_ref, keep_ref, send_refs):
    share = keep_ref.shape[0]
    keep_ref[...] = wide_ref[pl.ds(pl.multiple_of(own * share, share), share), :]
    for k, send_ref in enumerate(send_refs):
        at = pl.multiple_of((own ^ (k + 1)) * share, share)
        send_ref[:share, :] = wide_ref[pl.ds(at, share), :].astype(BF)


def allowed_pairs(columns, lines_ref):
    tokens = columns.shape[0]
    row_index = lax.broadcasted_iota(jnp.int32, (tokens, tokens), 0)
    column_index = lax.broadcasted_iota(jnp.int32, (tokens, tokens), 1)
    return (columns[:, 0:1] == lines_ref[0:1, :]) & (column_index <= row_index)


def weigh(queries, keys, allowed):
    scores = dot(queries, keys, 1, 1) * SCALE
    weights = jnp.where(allowed, 1.0 + scores + 0.5 * scores * scores, 0.0)
    return scores, weights, jnp.sum(weights, axis=1, keepdims=True)


def head_kernel(
    own_ref, packed_ref, wqk_ref, wvg_ref, taps_ref, lines_ref, out_w_ref,
    x_ref, turned_ref, root_ref, gain_ref, qk_ref, vg_ref,
    mixed_ref, attended_ref, gated_ref, keep_ref, *rest,
):
    send_refs, (shift_ref, wide_ref, normed_ref) = rest[:-3], rest[-3:]
    count, rows, tokens = packed_ref.shape
    share = rows - EXTRA
    width = count * share
    total = jnp.zeros((1, tokens), F32)
    for k in range(count):
        block = packed_ref[k, :share, :].astype(F32)
        total = total + jnp.sum(block * block, axis=0, keepdims=True)
    root = lax.rsqrt(total / width + epsilon)
    root_ref[...] = jnp.broadcast_to(root, root_ref.shape)
    for k in range(count):
        first = k * share
        turned = packed_ref[k, share:, :].astype(F32).T
        at = 0
        for piece in range(-(-share // tokens)):
            length = min(tokens, share - at)
            gain_ref[first + at : first + at + length, :] = turned[
                :length, 2 * piece : 2 * piece + 2
            ]
            at += length
        x_ref[first : first + share, :] = packed_ref[k, :share, :]
    for start in range(0, width, 256):
        block = slice(start, start + 256)
        piece = x_ref[block, :].astype(F32) * root * gain_ref[block, 0:1]
        turned_ref[block, :] = piece.astype(BF)
        normed_ref[:, block] = piece.T.astype(BF)
    normed = normed_ref[...]
    for k in range(2):
        vg_ref[k] = dot(normed, wvg_ref[k], 1, 1)
        qk_ref[k] = dot(normed, wqk_ref[k], 1, 1).astype(BF)
    heads = qk_ref.shape[2] // F
    size = share // heads
    taps = taps_ref[...].astype(F32)
    values = vg_ref[0]
    columns = lines_ref[...].T
    shift_ref[0:8, :] = jnp.zeros((8, share), F32)
    shift_ref[8 : 8 + tokens, :] = values
    summed = values * taps[0:1]
    for j in range(1, KERNEL):
        summed = summed + columns[:, j : j + 1] * (
            shift_ref[8 - j : 8 - j + tokens, :] * taps[j : j + 1]
        )
    mixed_ref[...] = summed.astype(BF)
    allowed = allowed_pairs(columns, lines_ref)
    for h in range(heads):
        feats = slice(h * F, (h + 1) * F)
        vals = slice(h * size, (h + 1) * size)
        _, weights, totals = weigh(qk_ref[0, :, feats], qk_ref[1, :, feats], allowed)
        attended_ref[:, vals] = dot((weights / totals).astype(BF), mixed_ref[:, vals])
    gates = vg_ref[1]
    gated = (attended_ref[...] * (gates * jax.nn.sigmoid(gates))).astype(BF)
    gated_ref[...] = gated
    for start in range(0, width, 256):
        wide_ref[start : start + 256, :] = dot(gated, out_w_ref[:, start : start + 256]).T
    send_blocks(own_ref[0], wide_ref, keep_ref, send_refs)


def ffn_kernel(
    own_ref, hidden_ref, gain_ref, gate_up_ref, down_ref, *rest,
):
    width, tokens = hidden_ref.shape
    count = width // rest[0].shape[0]
    cot_pieces, rest = rest[:count], rest[count:]
    cot_ref, turned_ref, root_ref, right_ref, keep_ref = rest[:5]
    send_refs, (normed_ref, wide_ref) = rest[5:-2], rest[-2:]
    step = pl.program_id(0)

    @pl.when(step == 0)
    def _():
        place_rows(own_ref[0], cot_ref, cot_pieces)
        total = jnp.zeros((1, tokens), F32)
        for start in range(0, width, 256):
            block = hidden_ref[start : start + 256, :].astype(F32)
            total = total + jnp.sum(block * block, axis=0, keepdims=True)
        root = lax.rsqrt(total / width + epsilon)
        root_ref[...] = jnp.broadcast_to(root, root_ref.shape)
        for start in range(0, width, 256):
            piece = (
                hidden_ref[start : start + 256, :].astype(F32)
                * root
                * gain_ref[start : start + 256, 1:2]
            )
            turned_ref[start : start + 256, :] = piece.astype(BF)
            normed_ref[:, start : start + 256] = piece.T.astype(BF)
            wide_ref[start : start + 256, :] = jnp.zeros((256, tokens), F32)

    normed = normed_ref[...]
    gate = dot(normed, gate_up_ref[0])
    up = dot(normed, gate_up_ref[1])
    d_act = dot(down_ref[...], cot_ref[...]).T
    logistic = jax.nn.sigmoid(gate)
    silu = gate * logistic
    right_ref[0] = (d_act * up * slope_of(gate, logistic)).astype(BF)
    right_ref[1] = (d_act * silu).astype(BF)
    right_ref[2] = (silu * up).astype(BF)
    for start in range(0, width, 256):
        rows = slice(start, start + 256)
        wide_ref[rows, :] = (
            wide_ref[rows, :]
            + dot(gate_up_ref[0, rows, :], right_ref[0], 1, 1)
            + dot(gate_up_ref[1, rows, :], right_ref[1], 1, 1)
        )

    @pl.when(step == pl.num_programs(0) - 1)
    def _():
        send_blocks(own_ref[0], wide_ref, keep_ref, send_refs)


def feed_kernel(own_ref, act_ref, down_ref, keep_ref, *rest):
    send_refs, (wide_ref,) = rest[:-1], rest[-1:]
    for start in range(0, wide_ref.shape[0], 256):
        wide_ref[start : start + 256, :] = dot(act_ref[0], down_ref[:, start : start + 256]).T
    send_blocks(own_ref[0], wide_ref, keep_ref, send_refs)


def add_kernel(count, *refs):
    keep_ref, arrived = refs[0], refs[1:count]
    out_ref, rounded_ref = refs[-2:]
    total = keep_ref[...]
    for ref in arrived:
        total = total + ref[...].astype(F32)
    out_ref[...] = total
    rounded_ref[...] = total.astype(BF)


def back_kernel(
    own_ref, hidden_ref, root_two_ref, gain_ref, cot_ref, x_ref, root_one_ref,
    out_w_ref, qk_ref, vg_ref, attended_ref, mixed_ref, taps_ref, lines_ref, wqk_ref, wvg_ref,
    gated_ref, *rest,
):
    width, tokens = hidden_ref.shape
    count = width // rest[0].shape[0]
    d_normed_pieces, rest = rest[:count], rest[count:]
    d_hidden_ref, branch_ref, delta_ref, small_ref, keep_ref, line_ref = rest[:6]
    send_refs, rest = rest[6 : 5 + count], rest[5 + count :]
    wide_ref, d_branch_ref, shift_ref, d_mixed_ref, d_normed_ref = rest
    place_rows(own_ref[0], d_normed_ref, d_normed_pieces)
    share = vg_ref.shape[2]
    heads = qk_ref.shape[2] // F
    size = share // heads
    own = own_ref[0]
    columns = lines_ref[...].T
    root_two = root_two_ref[0:1, :]
    total = jnp.zeros((1, tokens), F32)
    for start in range(0, width, 256):
        rows = slice(start, start + 256)
        unit = hidden_ref[rows, :].astype(F32) * root_two
        scaled = d_normed_ref[rows, :].astype(F32) * gain_ref[rows, 1:2]
        total = total + jnp.sum(scaled * unit, axis=0, keepdims=True)
    mean = total / width
    for start in range(0, width, 256):
        rows = slice(start, start + 256)
        unit = hidden_ref[rows, :].astype(F32) * root_two
        scaled = d_normed_ref[rows, :].astype(F32) * gain_ref[rows, 1:2]
        piece = cot_ref[rows, :].astype(F32) + root_two * (scaled - unit * mean)
        wide_ref[rows, :] = piece
        branch_ref[rows, :] = piece.astype(BF)
        d_branch_ref[:, rows] = piece.T.astype(BF)
    d_hidden_ref[...] = wide_ref[pl.ds(pl.multiple_of(own * share, share), share), :]
    d_gated = dot(d_branch_ref[...], out_w_ref[...], 1, 1)
    gates = vg_ref[1]
    logistic = jax.nn.sigmoid(gates)
    d_attended = (d_gated * (gates * logistic)).astype(BF)
    delta_ref[0, :, :share] = (d_gated * attended_ref[...] * slope_of(gates, logistic)).astype(BF)
    shift_ref[8 : 8 + tokens, :] = d_attended.astype(F32)
    allowed = allowed_pairs(columns, lines_ref)
    first = 2 * share
    last = first + 2 * heads * F
    delta_ref[0, :, last : last + share] = gated_ref[...]
    delta_ref[0, :, last + share :] = jnp.zeros((tokens, heads * F), BF)
    for h in range(heads):
        feats = slice(h * F, (h + 1) * F)
        vals = slice(h * size, (h + 1) * size)
        queries, keys = qk_ref[0, :, feats], qk_ref[1, :, feats]
        scores, weights, totals = weigh(queries, keys, allowed)
        probs = weights / totals
        d_att = shift_ref[8 : 8 + tokens, vals].astype(BF)
        d_mixed_ref[:, vals] = dot(probs.T.astype(BF), d_att)
        d_probs = dot(d_att, mixed_ref[:, vals], 1, 1)
        d_weights = (d_probs - jnp.sum(d_probs * probs, axis=1, keepdims=True)) / totals
        d_scores = jnp.where(allowed, d_weights * (1.0 + scores), 0.0)
        d_q = dot(d_scores.astype(BF), keys) * SCALE
        d_k = dot(d_scores.T.astype(BF), queries) * SCALE
        delta_ref[0, :, first + h * F : first + (h + 1) * F] = d_q.astype(BF)
        at = first + heads * F
        delta_ref[0, :, at + h * F : at + (h + 1) * F] = d_k.astype(BF)
    taps = taps_ref[...].astype(F32)
    d_mixed = d_mixed_ref[...]
    values = vg_ref[0]
    small_ref[...] = jnp.zeros(small_ref.shape, F32)
    small_ref[0:1, :] = jnp.sum(d_mixed * values, axis=0, keepdims=True)
    shift_ref[0:8, :] = jnp.zeros((8, share), F32)
    shift_ref[8 : 8 + tokens, :] = values
    for j in range(1, KERNEL):
        masked = columns[:, j : j + 1] * d_mixed
        small_ref[j : j + 1, :] = jnp.sum(
            masked * shift_ref[8 - j : 8 - j + tokens, :], axis=0, keepdims=True
        )
    d_values = d_mixed * taps[0:1]
    shift_ref[8 + tokens : 16 + tokens, :] = jnp.zeros((8, share), F32)
    for j in range(1, KERNEL):
        shift_ref[8 : 8 + tokens, :] = columns[:, j : j + 1] * d_mixed
        d_values = d_values + shift_ref[8 + j : 8 + j + tokens, :] * taps[j : j + 1]
    delta_ref[0, :, share : 2 * share] = d_values.astype(BF)
    d_gates = delta_ref[0, :, :share]
    d_values = delta_ref[0, :, share : 2 * share]
    d_queries = delta_ref[0, :, first : first + heads * F]
    d_keys = delta_ref[0, :, first + heads * F : first + 2 * heads * F]
    root_one = root_one_ref[0:1, :]
    line = jnp.zeros((1, tokens), F32)
    for start in range(0, width, 256):
        rows = slice(start, start + 256)
        piece = (
            dot(d_queries, wqk_ref[0, :, rows])
            + dot(d_keys, wqk_ref[1, :, rows])
            + dot(d_values, wvg_ref[0, :, rows])
            + dot(d_gates, wvg_ref[1, :, rows])
        ).T
        wide_ref[rows, :] = piece
        unit = x_ref[rows, :].astype(F32) * root_one
        line = line + jnp.sum(piece * (unit * gain_ref[rows, 0:1]), axis=0, keepdims=True)
    line_ref[...] = jnp.broadcast_to(line, line_ref.shape)
    send_blocks(own, wide_ref, keep_ref, send_refs)
    high = line.astype(BF)
    low = (line - high.astype(F32)).astype(BF)
    index = lax.broadcasted_iota(jnp.int32, (EXTRA, tokens), 0)
    extra = jnp.where(
        index == 0,
        jnp.broadcast_to(high.astype(F32), (EXTRA, tokens)),
        jnp.where(index == 1, jnp.broadcast_to(low.astype(F32), (EXTRA, tokens)), 0.0),
    ).astype(BF)
    for send_ref in send_refs:
        send_ref[share:, :] = extra


def merged(source):
    rows, columns = source.shape[-2:]
    return source.reshape(-1, rows, columns) if rows % 16 else source.reshape(1, -1, columns)


def product(lefts, rights, column, out_ref, at, size):
    sources = [merged(left) for left in lefts]
    rows = out_ref.shape[1]
    for k in range(sources[0].shape[0]):
        blocks = slice(None) if sources[0].shape[0] == 1 else slice(k, k + 1)
        value = dot(sources[0][k], rights[0][:, column : column + size])
        for source, right in zip(sources[1:], rights[1:]):
            value = value + dot(source[k], right[:, column : column + size])
        out_ref[blocks, :, at : at + size] = value.reshape(-1, rows, size).astype(BF)


def stage_kernel(orders, tile, where_ref, *refs):
    pairs, rights, outs = (refs[0:2], refs[2:4]), refs[4:6], refs[6:]
    per_slab = rights[0].shape[2]
    for p, order in enumerate(orders):
        for start in range(0, 3 * tile, 256):
            column = 3 * p * tile + start
            late = column >= 4 * tile
            lefts = [
                left[:, where_ref[1 + p], :, where_ref[0]]
                for left in (view_of(ref, order) for ref in pairs[int(late)])
            ]
            slab = [right[column // per_slab] for right in rights]
            product(lefts, slab, column % per_slab, outs[p], start, min(256, 3 * tile))


def view_of(ref, order):
    half, pair, rows, tokens = ref.shape
    low = 1 << (order[0] - 1)
    return ref.reshape(half // 2 // low, 2, low, pair, rows, tokens)


def path_orders(bits):
    return [list(range(1, bits)), list(reversed(range(1, bits)))]


def sum_rows(lefts, rights, tile, keep):
    count = lax.axis_size(DP)
    bits = count.bit_length() - 1
    width, tokens = lefts[0][0].shape
    rows = width // count
    orders = path_orders(bits)
    places = [own_bit(order[0]) for order in orders]
    if not keep:
        places = [1 - place for place in places]
    where = jnp.stack([own_bit(0)] + places).astype(jnp.int32)
    operands = [left.reshape(count // 2, 2, rows, tokens) for pair in lefts for left in pair]
    return pl.pallas_call(
        lambda *refs: stage_kernel(orders, tile, *refs),
        out_shape=[shaped(count // 4, rows, 3 * tile, dtype=BF)] * 2,
        in_specs=[scalars()] + [whole()] * 6,
        cost_estimate=cost(6 * width * tokens * tile, 6 * width * tile),
    )(where, *operands, *rights)


def third_kernel(count, where_ref, *refs):
    for p in range(count):
        kept, more = refs[2 * p : 2 * p + 2]
        outs = refs[2 * count + 2 * p : 2 * count + 2 * p + 2]
        for which, out_ref in enumerate(outs):
            place = where_ref[2 * p + which]
            total = kept[:, place].astype(F32) + more[:, place].astype(F32)
            out_ref[...] = total.astype(BF).reshape(out_ref.shape)


def sum_rows_third(sends, keeps):
    bits = lax.axis_size(DP).bit_length() - 1
    orders = path_orders(bits)
    remaining = [[bit for bit in reversed(range(1, bits)) if bit != order[0]] for order in orders]
    arrived = [swap_dp(send, order[0]) for order, send in zip(orders, sends)]
    for stage in range(1, bits - 1):
        operands, out_shape, places = [], [], []
        moved = 0
        for p, order in enumerate(orders):
            at = remaining[p].index(order[stage])
            low = 1 << (len(remaining[p]) - 1 - at)
            blocks, rows, size = keeps[p].shape
            high = blocks // (2 * low)
            remaining[p].pop(at)
            bit = own_bit(order[stage])
            places += [1 - bit, bit]
            operands += [each.reshape(high, 2, low, rows, size) for each in (keeps[p], arrived[p])]
            out_shape += [shaped(high * low, rows, size, dtype=BF)] * 2
            moved += 6 * blocks * rows * size
        outs = pl.pallas_call(
            lambda *refs: third_kernel(len(orders), *refs),
            out_shape=out_shape,
            in_specs=[scalars()] + [whole()] * len(operands),
            cost_estimate=cost(moved, moved),
        )(jnp.stack(places).astype(jnp.int32), *operands)
        sends, keeps = outs[0::2], outs[1::2]
        arrived = [swap_dp(send, order[stage]) for order, send in zip(orders, sends)]
    return [
        (keep.reshape(keep.shape[1:]), piece.reshape(piece.shape[1:]))
        for keep, piece in zip(keeps, arrived)
    ]


def advance_kernel(units, split, *refs):
    keep_a, more_a, keep_b, more_b, weight_ref, moment_ref, mean_ref = refs[:7]
    grad_ref, change_ref, moment_out_ref, mean_out_ref = refs[7:]
    rows = keep_a.shape[0]
    tiles = units // 128
    for column in range(0, 2 * units, 128):
        if column < units + split:
            tile = slice(column, column + 128)
            value = keep_a[:, tile].astype(F32) + more_a[:, tile].astype(F32)
        else:
            tile = slice(column - units - split, column - units - split + 128)
            value = keep_b[:, tile].astype(F32) + more_b[:, tile].astype(F32)
        at = (column % units) // 128 * 2 + column // units
        grad_ref[pl.ds(at, rows, stride=2 * tiles), :] = value
    change, moment, mean = advance(
        grad_ref[...], weight_ref[...], moment_ref[...], mean_ref[...]
    )
    change_ref[...] = change
    moment_out_ref[...] = moment
    mean_out_ref[...] = mean


def flattened(source):
    rows, pair, units = source.shape
    tiles = source.reshape(rows, pair, units // 128, 128).transpose(0, 2, 1, 3)
    return tiles.reshape(-1, 128)


def unflattened(source, units):
    tiles = source.reshape(-1, units // 128, 2, 128).transpose(0, 2, 1, 3)
    return tiles.reshape(-1, 2, units)


def advance_pairs(path_a, path_b, split, weight, moment, mean):
    rows, _, units = moment.shape
    step = 112 if rows % 112 == 0 else rows
    width = path_a[0].shape[1]
    flat = step * 2 * units // 128
    spec = pl.BlockSpec((flat, 128), lambda k: (k, 0))
    outs = pl.pallas_call(
        lambda *refs: advance_kernel(units, split, *refs),
        out_shape=[shaped(rows * 2 * units // 128, 128) for _ in range(4)],
        grid=(rows // step,),
        in_specs=[pl.BlockSpec((step, width), lambda k: (k, 0))] * 2
        + [pl.BlockSpec((step, units - split), lambda k: (k, 0))] * 2
        + [spec] * 3,
        out_specs=[spec] * 4,
        cost_estimate=cost(10 * rows * units, 64 * rows * units),
        name="adv",
    )(*path_a, *path_b, flattened(weight.astype(F32)), flattened(moment), flattened(mean))
    return [unflattened(out, units) for out in outs]


def last_kernel(share, width, *refs):
    keep_a, more_a, keep_b, more_b = refs[:4]
    pair_in, qk_in, out_in = refs[4:7], refs[7:10], refs[10:13]
    pair_out, qk_out, out_out = refs[13:17], refs[17:21], refs[21:25]
    whole_ref = refs[25]
    half = keep_a.shape[1]
    whole_ref[:, :half] = keep_a[...].astype(F32) + more_a[...].astype(F32)
    whole_ref[:, half:] = keep_b[...].astype(F32) + more_b[...].astype(F32)

    def step(grad, inputs, outputs, index):
        change, moment, mean = advance(grad, *(each[index] for each in inputs))
        for ref, value in zip(outputs, (grad, change, moment, mean)):
            ref[index] = value

    everything = (slice(None), slice(None))
    for which, start in ((0, share), (1, 0)):
        step(
            whole_ref[:, start : start + share], pair_in, pair_out,
            (slice(None), which, slice(None)),
        )
    first = 2 * share
    step(whole_ref[:, first : first + width].T, qk_in, qk_out, everything)
    first += width
    step(whole_ref[:, first : first + share].T, out_in, out_out, everything)


def local(
    inputs,
    cotangent,
    documents,
    gains,
    query_key,
    value_gate,
    conv_taps,
    output_weight,
    gate_up,
    down_weight,
    gains_moment,
    query_key_moment,
    value_gate_moment,
    conv_taps_moment,
    output_weight_moment,
    gate_up_moment,
    down_weight_moment,
    gains_mean,
    probe_lookup_smoothed,
    value_gate_mean,
    conv_taps_mean,
    output_weight_mean,
    gate_up_mean,
    down_weight_mean,
):
    tokens, share = inputs.shape
    groups = lax.axis_size(TENSOR)
    width = share * groups
    heads = H // groups
    key_width = heads * F
    hidden_units = down_weight.shape[0]
    own = lax.axis_index(TENSOR)
    own_index = own.astype(jnp.int32).reshape(1)

    inputs_turned = inputs.T
    pieces = -(-share // tokens)
    gain_lines = jnp.pad(gains, ((0, 0), (0, pieces * tokens - share)))
    gain_lines = gain_lines.reshape(2, pieces, tokens).transpose(1, 0, 2).reshape(-1, tokens)
    packed = jnp.concatenate(
        [inputs_turned, jnp.pad(gain_lines, ((0, EXTRA - 2 * pieces), (0, 0)))], axis=0
    )
    packed_whole = lax.all_gather(packed, TENSOR)
    documents_column = documents[:, None]
    lines = [documents.astype(F32)]
    for offset in range(1, KERNEL):
        earlier = jnp.pad(documents, (offset, 0), constant_values=-2)[:tokens]
        lines.append((earlier == documents).astype(F32))
    lines = jnp.pad(jnp.stack(lines), ((0, 8 - KERNEL), (0, 0)))
    masked = jnp.where(documents_column >= 0, cotangent, jnp.zeros_like(cotangent)).T
    masked, packed_whole = lax.optimization_barrier((masked, packed_whole))

    def sends(extra=0):
        return [shaped(share + extra, tokens, dtype=BF) for _ in range(groups - 1)]

    vmem = whole()
    query_key_rows = jnp.transpose(query_key, (1, 2, 0))
    value_gate_rows = jnp.transpose(value_gate, (1, 2, 0))
    cot_pieces = [masked] + [swap_tensor(masked, k) for k in range(1, groups)]
    (
        x_turned, normed_turned, root_one, gain_columns, projected, mixing,
        mixed_values, attended, gated, branch_keep, *branch_sends,
    ) = pl.pallas_call(
        head_kernel,
        out_shape=[
            shaped(width, tokens, dtype=BF),
            shaped(width, tokens, dtype=BF),
            shaped(8, tokens),
            shaped(width, 2),
            shaped(2, tokens, key_width, dtype=BF),
            shaped(2, tokens, share),
            shaped(tokens, share, dtype=BF),
            shaped(tokens, share),
            shaped(tokens, share, dtype=BF),
            shaped(share, tokens),
        ]
        + sends(),
        in_specs=[scalars()] + [vmem] * 6,
        scratch_shapes=[
            pltpu.VMEM((tokens + 16, share), F32),
            pltpu.VMEM((width, tokens), F32),
            pltpu.VMEM((tokens, width), BF),
        ],
        cost_estimate=cost(7 * tokens * share * width, 10 * share * width),
        name="head",
    )(
        own_index, packed_whole, query_key_rows, value_gate_rows, conv_taps, lines,
        output_weight,
    )
    normed_pair = (normed_turned, swap_dp(normed_turned, 0))
    arrived = [swap_tensor(send, k + 1) for k, send in enumerate(branch_sends)]
    gate_up_split = jnp.transpose(gate_up, (1, 0, 2))
    middle = hidden_units // 2
    dp_index = lax.axis_index(DP)
    dp_count = lax.axis_size(DP)

    def own_rows(source, axis_dim):
        length = source.shape[axis_dim] // dp_count
        return lax.dynamic_slice_in_dim(source, dp_index * length, length, axis_dim)

    own_weights = (
        own_rows(query_key, 0).astype(F32),
        own_rows(value_gate, 0).astype(F32),
        own_rows(output_weight, 1).astype(F32),
        own_rows(gate_up, 0).astype(F32),
        own_rows(down_weight, 1).astype(F32),
    )
    own_weights, branch_keep = lax.optimization_barrier((own_weights, branch_keep))
    own_query_key, own_value_gate, own_output_weight, own_gate_up, own_down_weight = own_weights
    hidden_own = inputs_turned.astype(F32) + branch_keep
    for piece in arrived:
        hidden_own = hidden_own + piece.astype(F32)
    hidden = lax.all_gather(hidden_own.astype(BF), TENSOR, axis=0, tiled=True)

    tile = 256
    cot_turned, normed_two_turned, root_two, ffn_right, keep_two, *sends_two = pl.pallas_call(
        ffn_kernel,
        out_shape=[
            shaped(width, tokens, dtype=BF),
            shaped(width, tokens, dtype=BF),
            shaped(8, tokens),
            shaped(3, tokens, hidden_units, dtype=BF),
            shaped(share, tokens),
        ]
        + sends(),
        grid=(hidden_units // tile,),
        in_specs=[
            scalars(),
            pl.BlockSpec((width, tokens), lambda f: (0, 0)),
            pl.BlockSpec((width, 2), lambda f: (0, 0)),
            pl.BlockSpec((2, width, tile), lambda f: (0, 0, f)),
            pl.BlockSpec((tile, width), lambda f: (f, 0)),
        ]
        + [pl.BlockSpec((share, tokens), lambda f: (0, 0))] * groups,
        out_specs=[
            pl.BlockSpec((width, tokens), lambda f: (0, 0)),
            pl.BlockSpec((width, tokens), lambda f: (0, 0)),
            pl.BlockSpec((8, tokens), lambda f: (0, 0)),
            pl.BlockSpec((3, tokens, tile), lambda f: (0, 0, f)),
            pl.BlockSpec((share, tokens), lambda f: (0, 0)),
        ]
        + [pl.BlockSpec((share, tokens), lambda f: (0, 0)) for _ in range(groups - 1)],
        scratch_shapes=[pltpu.VMEM((tokens, width), BF), pltpu.VMEM((width, tokens), F32)],
        cost_estimate=cost(10 * tokens * width * hidden_units, 6 * width * hidden_units),
        name="ffn",
    )(own_index, hidden, gain_columns, gate_up_split, down_weight, *cot_pieces)
    arrived_two = [swap_tensor(send, k + 1) for k, send in enumerate(sends_two)]

    middle = hidden_units // 2
    ffn_pairs = [(each, swap_dp(each, 0)) for each in (normed_two_turned, cot_turned, ffn_right)]
    ffn_group = (ffn_pairs[:2], ffn_pairs[2], hidden_units // 2)
    ffn_sends = sum_rows(*ffn_group, False)
    ffn_keeps = sum_rows(*ffn_group, True)

    d_normed_two_own, d_normed_two_rounded = pl.pallas_call(
        lambda *refs: add_kernel(groups, *refs),
        out_shape=[shaped(share, tokens), shaped(share, tokens, dtype=BF)],
        in_specs=[vmem] * groups + [pl.BlockSpec(memory_space=pl.ANY)] * 2,
        cost_estimate=cost(4 * share * tokens, 14 * share * tokens),
        name="add",
    )(keep_two, *arrived_two, *ffn_sends)
    d_normed_two_pieces = [d_normed_two_rounded] + [
        swap_tensor(d_normed_two_rounded, k) for k in range(1, groups)
    ]
    ffn_rows = sum_rows_third(ffn_sends, ffn_keeps)
    feed_keep, *feed_sends = pl.pallas_call(
        feed_kernel,
        out_shape=[shaped(share, tokens)] + sends(),
        grid=(1,),
        in_specs=[
            scalars(),
            pl.BlockSpec((1, tokens, hidden_units), lambda k: (2, 0, 0)),
            pl.BlockSpec((hidden_units, width), lambda k: (0, 0)),
        ],
        out_specs=[pl.BlockSpec((share, tokens), lambda k: (0, 0))] * groups,
        scratch_shapes=[pltpu.VMEM((width, tokens), F32)],
        cost_estimate=cost(2 * tokens * width * hidden_units, 2 * width * hidden_units),
        name="feed",
    )(own_index, ffn_right, down_weight)

    d_hidden_own, d_branch_turned, delta, taps_part, keep_one, line_one, *sends_one = (
        pl.pallas_call(
            back_kernel,
            out_shape=[
                shaped(share, tokens),
                shaped(width, tokens, dtype=BF),
                shaped(1, tokens, 3 * (share + key_width), dtype=BF),
                shaped(8, share),
                shaped(share, tokens),
                shaped(8, tokens),
            ]
            + sends(EXTRA),
            in_specs=[scalars()] + [vmem] * (16 + groups),
            scratch_shapes=[
                pltpu.VMEM((width, tokens), F32),
                pltpu.VMEM((tokens, width), BF),
                pltpu.VMEM((tokens + 16, share), F32),
                pltpu.VMEM((tokens, share), F32),
                pltpu.VMEM((width, tokens), BF),
            ],
            cost_estimate=cost(8 * tokens * width * share, 20 * width * share),
            name="back",
        )(
            own_index, hidden, root_two, gain_columns, cot_turned, x_turned,
            root_one, output_weight, projected, mixing, attended, mixed_values, conv_taps, lines,
            query_key_rows, value_gate_rows, gated, *d_normed_two_pieces,
        )
    )
    arrived_one = [swap_tensor(send, k + 1) for k, send in enumerate(sends_one)]
    all_columns = 2 * (share + key_width)
    mix_pairs = [normed_pair] + [(each, swap_dp(each, 0)) for each in (d_branch_turned, delta)]
    mix_group = (mix_pairs[:2], mix_pairs[2], all_columns // 4)
    mix_sends = sum_rows(*mix_group, False)
    mix_keeps = sum_rows(*mix_group, True)
    mix_rows = sum_rows_third(mix_sends, mix_keeps)

    feed_own = feed_keep
    feed_arrived = [swap_tensor(send, k + 1) for k, send in enumerate(feed_sends)]
    for piece in feed_arrived:
        feed_own = feed_own + piece.astype(F32)
    mixed = (hidden_own + feed_own).astype(BF).T

    def own_rows_of(source):
        return lax.dynamic_slice_in_dim(source, own * share, share, 0)

    gain_own = gains.astype(F32).T
    root_one_line, root_two_line = root_one[0:1], root_two[0:1]
    unit_two_own = own_rows_of(hidden).astype(F32) * root_two_line
    gain_two_grad = jnp.sum(d_normed_two_own * unit_two_own, axis=1)
    d_normed_own, line = keep_one, line_one[0:1]
    for piece in arrived_one:
        d_normed_own = d_normed_own + piece[:share].astype(F32)
        line = line + (piece[share : share + 1].astype(F32) + piece[share + 1 : share + 2].astype(F32))
    unit_one_own = inputs_turned.astype(F32) * root_one_line
    input_grad = (
        d_hidden_own
        + root_one_line * (d_normed_own * gain_own[:, 0:1] - unit_one_own * (line / width))
    ).T
    gain_one_grad = jnp.sum(d_normed_own * unit_one_own, axis=1)
    small = sum_dp(
        jnp.concatenate(
            [gain_one_grad[None], gain_two_grad[None], taps_part[:KERNEL], jnp.zeros((2, share))],
            axis=0,
        )
    )
    gains_grad = small[:2]
    conv_taps_grad = small[2 : 2 + KERNEL]
    down_weight_grad = sum(part[:, middle:].astype(F32) for part in ffn_rows[1]).T
    down_weight_grad = with_layout_constraint(
        lax.optimization_barrier(down_weight_grad), Layout(major_to_minor=(1, 0))
    )
    rows = width // lax.axis_size(DP)

    def turned_pairs(source):
        return source.transpose(1, 2, 0).reshape(2 * key_width, rows)

    last = pl.pallas_call(
        lambda *refs: last_kernel(share, 2 * key_width, *refs),
        out_shape=[shaped(rows, 2, share)] * 4
        + [shaped(2 * key_width, rows)] * 4
        + [shaped(share, rows)] * 4,
        in_specs=[vmem] * 13,
        scratch_shapes=[pltpu.VMEM((rows, 3 * (share + key_width)), F32)],
        cost_estimate=cost(30 * rows * share, 100 * rows * share),
        name="last",
    )(
        *mix_rows[0], *mix_rows[1],
        own_value_gate, value_gate_moment, value_gate_mean,
        turned_pairs(own_query_key), turned_pairs(query_key_moment),
        turned_pairs(probe_lookup_smoothed),
        own_output_weight, output_weight_moment, output_weight_mean,
    )
    value_gate_grad, value_gate_change, value_gate_momentum, value_gate_average = last[:4]
    query_key_grad, query_key_change, query_key_momentum, query_key_average = [
        each.reshape(2, key_width, rows).transpose(2, 0, 1) for each in last[4:8]
    ]
    (
        output_weight_grad, output_weight_change, output_weight_momentum,
        output_weight_average,
    ) = last[8:]
    gains_change, gains_momentum, gains_average = advance(
        gains_grad, gains, gains_moment, gains_mean
    )
    conv_taps_change, conv_taps_momentum, conv_taps_average = advance(
        conv_taps_grad, conv_taps, conv_taps_moment, conv_taps_mean
    )
    gate_up_grad, gate_up_change, gate_up_momentum, gate_up_average = advance_pairs(
        *ffn_rows, middle, own_gate_up, gate_up_moment, gate_up_mean
    )
    down_weight_change, down_weight_momentum, down_weight_average = advance(
        down_weight_grad, own_down_weight, down_weight_moment, down_weight_mean
    )
    return (
        mixed,
        input_grad,
        gains_grad,
        query_key_grad,
        value_gate_grad,
        conv_taps_grad,
        output_weight_grad,
        gate_up_grad,
        down_weight_grad,
        gains_change,
        query_key_change,
        value_gate_change,
        conv_taps_change,
        output_weight_change,
        gate_up_change,
        down_weight_change,
        gains_momentum,
        query_key_momentum,
        value_gate_momentum,
        conv_taps_momentum,
        output_weight_momentum,
        gate_up_momentum,
        down_weight_momentum,
        gains_average,
        query_key_average,
        value_gate_average,
        conv_taps_average,
        output_weight_average,
        gate_up_average,
        down_weight_average,
    )


def solution(mesh):
    return jax.shard_map(
        local,
        mesh=mesh,
        in_specs=(
            P(DP, TENSOR),
            P(DP, TENSOR),
            P(DP),
            P(None, TENSOR),
            P(None, None, TENSOR),
            P(None, None, TENSOR),
            P(None, TENSOR),
            P(TENSOR, None),
            P(None, None, TENSOR),
            P(TENSOR, None),
            P(None, TENSOR),
            P(DP, None, TENSOR),
            P(DP, None, TENSOR),
            P(None, TENSOR),
            P(TENSOR, DP),
            P(DP, None, TENSOR),
            P(TENSOR, DP),
            P(None, TENSOR),
            P(DP, None, TENSOR),
            P(DP, None, TENSOR),
            P(None, TENSOR),
            P(TENSOR, DP),
            P(DP, None, TENSOR),
            P(TENSOR, DP),
        ),
        out_specs=(
            P(DP, TENSOR),
            P(DP, TENSOR),
            P(None, TENSOR),
            P(DP, None, TENSOR),
            P(DP, None, TENSOR),
            P(None, TENSOR),
            P(TENSOR, DP),
            P(DP, None, TENSOR),
            P(TENSOR, DP),
            P(None, TENSOR),
            P(DP, None, TENSOR),
            P(DP, None, TENSOR),
            P(None, TENSOR),
            P(TENSOR, DP),
            P(DP, None, TENSOR),
            P(TENSOR, DP),
            P(None, TENSOR),
            P(DP, None, TENSOR),
            P(DP, None, TENSOR),
            P(None, TENSOR),
            P(TENSOR, DP),
            P(DP, None, TENSOR),
            P(TENSOR, DP),
            P(None, TENSOR),
            P(DP, None, TENSOR),
            P(DP, None, TENSOR),
            P(None, TENSOR),
            P(TENSOR, DP),
            P(DP, None, TENSOR),
            P(TENSOR, DP),
        ),
        check_vma=False,
    )
```

```python
import math

import jax
import jax.numpy as jnp
from jax import lax
from jax.experimental import pallas as pl
from jax.experimental.pallas import tpu as pltpu
from jax.experimental.layout import Layout, with_layout_constraint
from jax.sharding import PartitionSpec as P

H = 16
F = 16
KERNEL = 4
EXTRA = 16


DP = "dp"
TENSOR = "tensor"

epsilon = 1e-06
momentum_decay = 0.9
learning_rate = 0.001
average_rate = 0.1

BF = jnp.bfloat16
F32 = jnp.float32
SCALE = 1.0 / math.sqrt(F)


def advance(grad, weight, moment, average):
    moment_new = momentum_decay * moment + (1.0 - momentum_decay) * grad
    change = -learning_rate * ((1.0 - momentum_decay) * grad + momentum_decay * moment_new)
    average_new = average + average_rate * (weight.astype(jnp.float32) + change - average)
    return (change, moment_new, average_new)


def shaped(*shape, dtype=F32):
    return jax.ShapeDtypeStruct(shape, dtype)


def whole():
    return pl.BlockSpec(memory_space=pltpu.VMEM)


def scalars():
    return pl.BlockSpec(memory_space=pltpu.SMEM)


def cost(flops, moved):
    return pl.CostEstimate(flops=int(flops), transcendentals=0, bytes_accessed=int(moved))


def dot(left, right, left_dim=1, right_dim=0):
    return lax.dot_general(
        left, right, (((left_dim,), (right_dim,)), ((), ())), preferred_element_type=F32
    )


def slope_of(argument, logistic):
    return logistic * (1.0 + argument * (1.0 - logistic))


def own_bit(bit):
    return (lax.axis_index(DP) >> bit) & 1


def swap_dp(source, bit):
    count = lax.axis_size(DP)
    return lax.ppermute(source, DP, [(k, k ^ (1 << bit)) for k in range(count)])


def swap_tensor(source, distance):
    count = lax.axis_size(TENSOR)
    return lax.ppermute(source, TENSOR, [(k, k ^ distance) for k in range(count)])


def sum_dp(source):
    for bit in range(lax.axis_size(DP).bit_length() - 1):
        arrived = swap_dp(source, bit)
        source = source + arrived
    return source


def place_rows(own, whole_ref, pieces):
    share = pieces[0].shape[0]
    for k, piece in enumerate(pieces):
        at = pl.multiple_of((own ^ k) * share, share)
        whole_ref[pl.ds(at, share), :] = piece[...]


def send_blocks(own, wide_ref, keep_ref, send_refs):
    share = keep_ref.shape[0]
    keep_ref[...] = wide_ref[pl.ds(pl.multiple_of(own * share, share), share), :]
    for k, send_ref in enumerate(send_refs):
        at = pl.multiple_of((own ^ (k + 1)) * share, share)
        send_ref[:share, :] = wide_ref[pl.ds(at, share), :].astype(BF)


def allowed_pairs(columns, lines_ref):
    tokens = columns.shape[0]
    row_index = lax.broadcasted_iota(jnp.int32, (tokens, tokens), 0)
    column_index = lax.broadcasted_iota(jnp.int32, (tokens, tokens), 1)
    return (columns[:, 0:1] == lines_ref[0:1, :]) & (column_index <= row_index)


def weigh(queries, keys, allowed):
    scores = dot(queries, keys, 1, 1) * SCALE
    weights = jnp.where(allowed, 1.0 + scores + 0.5 * scores * scores, 0.0)
    return scores, weights, jnp.sum(weights, axis=1, keepdims=True)


def head_kernel(
    own_ref, packed_ref, wqk_ref, wvg_ref, taps_ref, lines_ref, out_w_ref,
    x_ref, turned_ref, root_ref, gain_ref, qk_ref, vg_ref,
    mixed_ref, attended_ref, gated_ref, keep_ref, *rest,
):
    send_refs, (shift_ref, wide_ref, normed_ref) = rest[:-3], rest[-3:]
    count, rows, tokens = packed_ref.shape
    share = rows - EXTRA
    width = count * share
    total = jnp.zeros((1, tokens), F32)
    for k in range(count):
        block = packed_ref[k, :share, :].astype(F32)
        total = total + jnp.sum(block * block, axis=0, keepdims=True)
    root = lax.rsqrt(total / width + epsilon)
    root_ref[...] = jnp.broadcast_to(root, root_ref.shape)
    for k in range(count):
        first = k * share
        turned = packed_ref[k, share:, :].astype(F32).T
        at = 0
        for piece in range(-(-share // tokens)):
            length = min(tokens, share - at)
            gain_ref[first + at : first + at + length, :] = turned[
                :length, 2 * piece : 2 * piece + 2
            ]
            at += length
        x_ref[first : first + share, :] = packed_ref[k, :share, :]
    for start in range(0, width, 256):
        block = slice(start, start + 256)
        piece = x_ref[block, :].astype(F32) * root * gain_ref[block, 0:1]
        turned_ref[block, :] = piece.astype(BF)
        normed_ref[:, block] = piece.T.astype(BF)
    normed = normed_ref[...]
    for k in range(2):
        vg_ref[k] = dot(normed, wvg_ref[k], 1, 1)
        qk_ref[k] = dot(normed, wqk_ref[k], 1, 1).astype(BF)
    heads = qk_ref.shape[2] // F
    size = share // heads
    taps = taps_ref[...].astype(F32)
    values = vg_ref[0]
    columns = lines_ref[...].T
    shift_ref[0:8, :] = jnp.zeros((8, share), F32)
    shift_ref[8 : 8 + tokens, :] = values
    summed = values * taps[0:1]
    for j in range(1, KERNEL):
        summed = summed + columns[:, j : j + 1] * (
            shift_ref[8 - j : 8 - j + tokens, :] * taps[j : j + 1]
        )
    mixed_ref[...] = summed.astype(BF)
    allowed = allowed_pairs(columns, lines_ref)
    for h in range(heads):
        feats = slice(h * F, (h + 1) * F)
        vals = slice(h * size, (h + 1) * size)
        _, weights, totals = weigh(qk_ref[0, :, feats], qk_ref[1, :, feats], allowed)
        attended_ref[:, vals] = dot((weights * (1.0 / totals)).astype(BF), mixed_ref[:, vals])
    gates = vg_ref[1]
    gated = (attended_ref[...] * (gates * jax.nn.sigmoid(gates))).astype(BF)
    gated_ref[...] = gated
    for start in range(0, width, 256):
        wide_ref[start : start + 256, :] = dot(gated, out_w_ref[:, start : start + 256]).T
    send_blocks(own_ref[0], wide_ref, keep_ref, send_refs)


def ffn_kernel(
    own_ref, hidden_ref, gain_ref, gate_up_ref, down_ref, *rest,
):
    width, tokens = hidden_ref.shape
    count = width // rest[0].shape[0]
    cot_pieces, rest = rest[:count], rest[count:]
    cot_ref, turned_ref, root_ref, right_ref, keep_ref = rest[:5]
    send_refs, (normed_ref, wide_ref) = rest[5:-2], rest[-2:]
    tile = 512
    place_rows(own_ref[0], cot_ref, cot_pieces)
    total = jnp.zeros((1, tokens), F32)
    for start in range(0, width, 256):
        block = hidden_ref[start : start + 256, :].astype(F32)
        total = total + jnp.sum(block * block, axis=0, keepdims=True)
    root = lax.rsqrt(total / width + epsilon)
    root_ref[...] = jnp.broadcast_to(root, root_ref.shape)
    for start in range(0, width, 256):
        rows = slice(start, start + 256)
        piece = hidden_ref[rows, :].astype(F32) * root * gain_ref[rows, 1:2]
        turned_ref[rows, :] = piece.astype(BF)
        normed_ref[:, rows] = piece.T.astype(BF)
        wide_ref[rows, :] = jnp.zeros((256, tokens), F32)

    @pl.loop(0, down_ref.shape[0] // tile)
    def _(step):
        units = pl.ds(pl.multiple_of(step * tile, tile), tile)
        gate = dot(normed_ref[...], gate_up_ref[0, :, units])
        up = dot(normed_ref[...], gate_up_ref[1, :, units])
        d_act = dot(down_ref[units, :], cot_ref[...]).T
        logistic = jax.nn.sigmoid(gate)
        silu = gate * logistic
        right_ref[0, :, units] = (d_act * up * slope_of(gate, logistic)).astype(BF)
        right_ref[1, :, units] = (d_act * silu).astype(BF)
        right_ref[2, :, units] = (silu * up).astype(BF)
        wide_ref[...] = (
            wide_ref[...]
            + dot(gate_up_ref[0, :, units], right_ref[0, :, units], 1, 1)
            + dot(gate_up_ref[1, :, units], right_ref[1, :, units], 1, 1)
        )

    send_blocks(own_ref[0], wide_ref, keep_ref, send_refs)


def feed_kernel(own_ref, act_ref, down_ref, keep_ref, *rest):
    send_refs, (wide_ref,) = rest[:-1], rest[-1:]
    for start in range(0, wide_ref.shape[0], 256):
        wide_ref[start : start + 256, :] = dot(act_ref[0], down_ref[:, start : start + 256]).T
    send_blocks(own_ref[0], wide_ref, keep_ref, send_refs)


def add_kernel(count, *refs):
    keep_ref, arrived = refs[0], refs[1:count]
    out_ref, rounded_ref = refs[-2:]
    total = keep_ref[...]
    for ref in arrived:
        total = total + ref[...].astype(F32)
    out_ref[...] = total
    rounded_ref[...] = total.astype(BF)


def back_kernel(
    own_ref, hidden_ref, root_two_ref, gain_ref, cot_ref, x_ref, root_one_ref,
    out_w_ref, qk_ref, vg_ref, attended_ref, mixed_ref, taps_ref, lines_ref, wqk_ref, wvg_ref,
    gated_ref, *rest,
):
    width, tokens = hidden_ref.shape
    count = width // rest[0].shape[0]
    d_normed_pieces, rest = rest[:count], rest[count:]
    d_hidden_ref, branch_ref, delta_ref, small_ref, keep_ref, line_ref = rest[:6]
    send_refs, rest = rest[6 : 5 + count], rest[5 + count :]
    wide_ref, d_branch_ref, shift_ref, d_mixed_ref, d_normed_ref = rest
    place_rows(own_ref[0], d_normed_ref, d_normed_pieces)
    share = vg_ref.shape[2]
    heads = qk_ref.shape[2] // F
    size = share // heads
    own = own_ref[0]
    columns = lines_ref[...].T
    root_two = root_two_ref[0:1, :]
    total = jnp.zeros((1, tokens), F32)
    for start in range(0, width, 256):
        rows = slice(start, start + 256)
        unit = hidden_ref[rows, :].astype(F32) * root_two
        scaled = d_normed_ref[rows, :].astype(F32) * gain_ref[rows, 1:2]
        total = total + jnp.sum(scaled * unit, axis=0, keepdims=True)
    mean = total / width
    for start in range(0, width, 256):
        rows = slice(start, start + 256)
        unit = hidden_ref[rows, :].astype(F32) * root_two
        scaled = d_normed_ref[rows, :].astype(F32) * gain_ref[rows, 1:2]
        piece = cot_ref[rows, :].astype(F32) + root_two * (scaled - unit * mean)
        wide_ref[rows, :] = piece
        branch_ref[rows, :] = piece.astype(BF)
        d_branch_ref[:, rows] = piece.T.astype(BF)
    d_hidden_ref[...] = wide_ref[pl.ds(pl.multiple_of(own * share, share), share), :]
    d_gated = dot(d_branch_ref[...], out_w_ref[...], 1, 1)
    gates = vg_ref[1]
    logistic = jax.nn.sigmoid(gates)
    d_attended = (d_gated * (gates * logistic)).astype(BF)
    delta_ref[0, :, :share] = (d_gated * attended_ref[...] * slope_of(gates, logistic)).astype(BF)
    shift_ref[8 : 8 + tokens, :] = d_attended.astype(F32)
    allowed = allowed_pairs(columns, lines_ref)
    first = 2 * share
    last = first + 2 * heads * F
    delta_ref[0, :, last : last + share] = gated_ref[...]
    delta_ref[0, :, last + share :] = jnp.zeros((tokens, heads * F), BF)
    for h in range(heads):
        feats = slice(h * F, (h + 1) * F)
        vals = slice(h * size, (h + 1) * size)
        queries, keys = qk_ref[0, :, feats], qk_ref[1, :, feats]
        scores, weights, totals = weigh(queries, keys, allowed)
        inverse = 1.0 / totals
        probs = weights * inverse
        d_att = shift_ref[8 : 8 + tokens, vals].astype(BF)
        d_mixed_ref[:, vals] = dot(probs.T.astype(BF), d_att)
        d_probs = dot(d_att, mixed_ref[:, vals], 1, 1)
        d_weights = (d_probs - jnp.sum(d_probs * probs, axis=1, keepdims=True)) * inverse
        d_scores = jnp.where(allowed, d_weights * (1.0 + scores), 0.0)
        d_q = dot(d_scores.astype(BF), keys) * SCALE
        d_k = dot(d_scores.T.astype(BF), queries) * SCALE
        delta_ref[0, :, first + h * F : first + (h + 1) * F] = d_q.astype(BF)
        at = first + heads * F
        delta_ref[0, :, at + h * F : at + (h + 1) * F] = d_k.astype(BF)
    taps = taps_ref[...].astype(F32)
    d_mixed = d_mixed_ref[...]
    values = vg_ref[0]
    small_ref[...] = jnp.zeros(small_ref.shape, F32)
    small_ref[0:1, :] = jnp.sum(d_mixed * values, axis=0, keepdims=True)
    shift_ref[0:8, :] = jnp.zeros((8, share), F32)
    shift_ref[8 : 8 + tokens, :] = values
    for j in range(1, KERNEL):
        masked = columns[:, j : j + 1] * d_mixed
        small_ref[j : j + 1, :] = jnp.sum(
            masked * shift_ref[8 - j : 8 - j + tokens, :], axis=0, keepdims=True
        )
    d_values = d_mixed * taps[0:1]
    shift_ref[8 + tokens : 16 + tokens, :] = jnp.zeros((8, share), F32)
    for j in range(1, KERNEL):
        shift_ref[8 : 8 + tokens, :] = columns[:, j : j + 1] * d_mixed
        d_values = d_values + shift_ref[8 + j : 8 + j + tokens, :] * taps[j : j + 1]
    delta_ref[0, :, share : 2 * share] = d_values.astype(BF)
    d_gates = delta_ref[0, :, :share]
    d_values = delta_ref[0, :, share : 2 * share]
    d_queries = delta_ref[0, :, first : first + heads * F]
    d_keys = delta_ref[0, :, first + heads * F : first + 2 * heads * F]
    root_one = root_one_ref[0:1, :]
    line = jnp.zeros((1, tokens), F32)
    for start in range(0, width, 256):
        rows = slice(start, start + 256)
        piece = (
            dot(d_queries, wqk_ref[0, :, rows])
            + dot(d_keys, wqk_ref[1, :, rows])
            + dot(d_values, wvg_ref[0, :, rows])
            + dot(d_gates, wvg_ref[1, :, rows])
        ).T
        wide_ref[rows, :] = piece
        unit = x_ref[rows, :].astype(F32) * root_one
        line = line + jnp.sum(piece * (unit * gain_ref[rows, 0:1]), axis=0, keepdims=True)
    line_ref[...] = jnp.broadcast_to(line, line_ref.shape)
    send_blocks(own, wide_ref, keep_ref, send_refs)
    high = line.astype(BF)
    low = (line - high.astype(F32)).astype(BF)
    index = lax.broadcasted_iota(jnp.int32, (EXTRA, tokens), 0)
    extra = jnp.where(
        index == 0,
        jnp.broadcast_to(high.astype(F32), (EXTRA, tokens)),
        jnp.where(index == 1, jnp.broadcast_to(low.astype(F32), (EXTRA, tokens)), 0.0),
    ).astype(BF)
    for send_ref in send_refs:
        send_ref[share:, :] = extra


def merged(source):
    rows, columns = source.shape[-2:]
    return source.reshape(-1, rows, columns) if rows % 16 else source.reshape(1, -1, columns)


def product(lefts, rights, column, out_ref, at, size):
    sources = [merged(left) for left in lefts]
    rows = out_ref.shape[1]
    for k in range(sources[0].shape[0]):
        blocks = slice(None) if sources[0].shape[0] == 1 else slice(k, k + 1)
        value = dot(sources[0][k], rights[0][:, column : column + size])
        for source, right in zip(sources[1:], rights[1:]):
            value = value + dot(source[k], right[:, column : column + size])
        out_ref[blocks, :, at : at + size] = value.reshape(-1, rows, size).astype(BF)


def stage_kernel(orders, tile, where_ref, *refs):
    pairs, rights, outs = (refs[0:2], refs[2:4]), refs[4:6], refs[6:]
    per_slab = rights[0].shape[2]
    for p, order in enumerate(orders):
        for start in range(0, 3 * tile, 256):
            column = 3 * p * tile + start
            late = column >= 4 * tile
            lefts = [
                left[:, where_ref[1 + p], :, where_ref[0]]
                for left in (view_of(ref, order) for ref in pairs[int(late)])
            ]
            slab = [right[column // per_slab] for right in rights]
            product(lefts, slab, column % per_slab, outs[p], start, min(256, 3 * tile))


def view_of(ref, order):
    half, pair, rows, tokens = ref.shape
    low = 1 << (order[0] - 1)
    return ref.reshape(half // 2 // low, 2, low, pair, rows, tokens)


def path_orders(bits):
    return [list(range(1, bits)), list(reversed(range(1, bits)))]


def sum_rows(lefts, rights, tile, keep):
    count = lax.axis_size(DP)
    bits = count.bit_length() - 1
    width, tokens = lefts[0][0].shape
    rows = width // count
    orders = path_orders(bits)
    places = [own_bit(order[0]) for order in orders]
    if not keep:
        places = [1 - place for place in places]
    where = jnp.stack([own_bit(0)] + places).astype(jnp.int32)
    operands = [left.reshape(count // 2, 2, rows, tokens) for pair in lefts for left in pair]
    return pl.pallas_call(
        lambda *refs: stage_kernel(orders, tile, *refs),
        out_shape=[shaped(count // 4, rows, 3 * tile, dtype=BF)] * 2,
        in_specs=[scalars()] + [whole()] * 6,
        cost_estimate=cost(6 * width * tokens * tile, 6 * width * tile),
    )(where, *operands, *rights)


def third_kernel(count, where_ref, *refs):
    for p in range(count):
        kept, more = refs[2 * p : 2 * p + 2]
        outs = refs[2 * count + 2 * p : 2 * count + 2 * p + 2]
        for which, out_ref in enumerate(outs):
            place = where_ref[2 * p + which]
            total = kept[:, place].astype(F32) + more[:, place].astype(F32)
            out_ref[...] = total.astype(BF).reshape(out_ref.shape)


def sum_rows_third(sends, keeps):
    bits = lax.axis_size(DP).bit_length() - 1
    orders = path_orders(bits)
    remaining = [[bit for bit in reversed(range(1, bits)) if bit != order[0]] for order in orders]
    arrived = [swap_dp(send, order[0]) for order, send in zip(orders, sends)]
    for stage in range(1, bits - 1):
        operands, out_shape, places = [], [], []
        moved = 0
        for p, order in enumerate(orders):
            at = remaining[p].index(order[stage])
            low = 1 << (len(remaining[p]) - 1 - at)
            blocks, rows, size = keeps[p].shape
            high = blocks // (2 * low)
            remaining[p].pop(at)
            bit = own_bit(order[stage])
            places += [1 - bit, bit]
            operands += [each.reshape(high, 2, low, rows, size) for each in (keeps[p], arrived[p])]
            out_shape += [shaped(high * low, rows, size, dtype=BF)] * 2
            moved += 6 * blocks * rows * size
        outs = pl.pallas_call(
            lambda *refs: third_kernel(len(orders), *refs),
            out_shape=out_shape,
            in_specs=[scalars()] + [whole()] * len(operands),
            cost_estimate=cost(moved, moved),
        )(jnp.stack(places).astype(jnp.int32), *operands)
        sends, keeps = outs[0::2], outs[1::2]
        arrived = [swap_dp(send, order[stage]) for order, send in zip(orders, sends)]
    return [
        (keep.reshape(keep.shape[1:]), piece.reshape(piece.shape[1:]))
        for keep, piece in zip(keeps, arrived)
    ]


def advance_kernel(units, split, *refs):
    keep_a, more_a, keep_b, more_b, weight_ref, moment_ref, mean_ref = refs[:7]
    grad_ref, change_ref, moment_out_ref, mean_out_ref = refs[7:]
    rows = keep_a.shape[0]
    tiles = units // 128
    for column in range(0, 2 * units, 128):
        if column < units + split:
            tile = slice(column, column + 128)
            value = keep_a[:, tile].astype(F32) + more_a[:, tile].astype(F32)
        else:
            tile = slice(column - units - split, column - units - split + 128)
            value = keep_b[:, tile].astype(F32) + more_b[:, tile].astype(F32)
        at = (column % units) // 128 * 2 + column // units
        grad_ref[pl.ds(at, rows, stride=2 * tiles), :] = value
    change, moment, mean = advance(
        grad_ref[...], weight_ref[...], moment_ref[...], mean_ref[...]
    )
    change_ref[...] = change
    moment_out_ref[...] = moment
    mean_out_ref[...] = mean


def flattened(source):
    rows, pair, units = source.shape
    tiles = source.reshape(rows, pair, units // 128, 128).transpose(0, 2, 1, 3)
    return tiles.reshape(-1, 128)


def unflattened(source, units):
    tiles = source.reshape(-1, units // 128, 2, 128).transpose(0, 2, 1, 3)
    return tiles.reshape(-1, 2, units)


def advance_pairs(path_a, path_b, split, weight, moment, mean):
    rows, _, units = moment.shape
    step = 112 if rows % 112 == 0 else rows
    width = path_a[0].shape[1]
    flat = step * 2 * units // 128
    spec = pl.BlockSpec((flat, 128), lambda k: (k, 0))
    outs = pl.pallas_call(
        lambda *refs: advance_kernel(units, split, *refs),
        out_shape=[shaped(rows * 2 * units // 128, 128) for _ in range(4)],
        grid=(rows // step,),
        in_specs=[pl.BlockSpec((step, width), lambda k: (k, 0))] * 2
        + [pl.BlockSpec((step, units - split), lambda k: (k, 0))] * 2
        + [spec] * 3,
        out_specs=[spec] * 4,
        cost_estimate=cost(10 * rows * units, 64 * rows * units),
        name="adv",
    )(*path_a, *path_b, flattened(weight.astype(F32)), flattened(moment), flattened(mean))
    return [unflattened(out, units) for out in outs]


def last_kernel(share, width, *refs):
    keep_a, more_a, keep_b, more_b = refs[:4]
    pair_in, qk_in, out_in = refs[4:7], refs[7:10], refs[10:13]
    pair_out, qk_out, out_out = refs[13:17], refs[17:21], refs[21:25]
    whole_ref = refs[25]
    half = keep_a.shape[1]
    whole_ref[:, :half] = keep_a[...].astype(F32) + more_a[...].astype(F32)
    whole_ref[:, half:] = keep_b[...].astype(F32) + more_b[...].astype(F32)

    def step(grad, inputs, outputs, index):
        change, moment, mean = advance(grad, *(each[index] for each in inputs))
        for ref, value in zip(outputs, (grad, change, moment, mean)):
            ref[index] = value

    everything = (slice(None), slice(None))
    for which, start in ((0, share), (1, 0)):
        step(
            whole_ref[:, start : start + share], pair_in, pair_out,
            (slice(None), which, slice(None)),
        )
    first = 2 * share
    step(whole_ref[:, first : first + width].T, qk_in, qk_out, everything)
    first += width
    step(whole_ref[:, first : first + share].T, out_in, out_out, everything)


def local(
    inputs,
    cotangent,
    documents,
    gains,
    query_key,
    value_gate,
    conv_taps,
    output_weight,
    gate_up,
    down_weight,
    gains_moment,
    query_key_moment,
    value_gate_moment,
    conv_taps_moment,
    output_weight_moment,
    gate_up_moment,
    down_weight_moment,
    gains_mean,
    probe_lookup_smoothed,
    value_gate_mean,
    conv_taps_mean,
    output_weight_mean,
    gate_up_mean,
    down_weight_mean,
):
    tokens, share = inputs.shape
    groups = lax.axis_size(TENSOR)
    width = share * groups
    heads = H // groups
    key_width = heads * F
    hidden_units = down_weight.shape[0]
    own = lax.axis_index(TENSOR)
    own_index = own.astype(jnp.int32).reshape(1)

    inputs_turned = inputs.T
    pieces = -(-share // tokens)
    gain_lines = jnp.pad(gains, ((0, 0), (0, pieces * tokens - share)))
    gain_lines = gain_lines.reshape(2, pieces, tokens).transpose(1, 0, 2).reshape(-1, tokens)
    packed = jnp.concatenate(
        [inputs_turned, jnp.pad(gain_lines, ((0, EXTRA - 2 * pieces), (0, 0)))], axis=0
    )
    documents_column = documents[:, None]
    masked = jnp.where(documents_column >= 0, cotangent, jnp.zeros_like(cotangent)).T
    masked, packed = lax.optimization_barrier((masked, packed))
    packed_whole = lax.all_gather(packed, TENSOR)
    lines = [documents.astype(F32)]
    for offset in range(1, KERNEL):
        earlier = jnp.pad(documents, (offset, 0), constant_values=-2)[:tokens]
        lines.append((earlier == documents).astype(F32))
    lines = jnp.pad(jnp.stack(lines), ((0, 8 - KERNEL), (0, 0)))
    masked, packed_whole = lax.optimization_barrier((masked, packed_whole))

    def sends(extra=0):
        return [shaped(share + extra, tokens, dtype=BF) for _ in range(groups - 1)]

    vmem = whole()
    query_key_rows = jnp.transpose(query_key, (1, 2, 0))
    value_gate_rows = jnp.transpose(value_gate, (1, 2, 0))
    cot_pieces = [masked] + [swap_tensor(masked, k) for k in range(1, groups)]
    (
        x_turned, normed_turned, root_one, gain_columns, projected, mixing,
        mixed_values, attended, gated, branch_keep, *branch_sends,
    ) = pl.pallas_call(
        head_kernel,
        out_shape=[
            shaped(width, tokens, dtype=BF),
            shaped(width, tokens, dtype=BF),
            shaped(8, tokens),
            shaped(width, 2),
            shaped(2, tokens, key_width, dtype=BF),
            shaped(2, tokens, share),
            shaped(tokens, share, dtype=BF),
            shaped(tokens, share),
            shaped(tokens, share, dtype=BF),
            shaped(share, tokens),
        ]
        + sends(),
        in_specs=[scalars()] + [vmem] * 6,
        scratch_shapes=[
            pltpu.VMEM((tokens + 16, share), F32),
            pltpu.VMEM((width, tokens), F32),
            pltpu.VMEM((tokens, width), BF),
        ],
        cost_estimate=cost(7 * tokens * share * width, 10 * share * width),
        name="head",
    )(
        own_index, packed_whole, query_key_rows, value_gate_rows, conv_taps, lines,
        output_weight,
    )
    normed_pair = (normed_turned, swap_dp(normed_turned, 0))
    arrived = [swap_tensor(send, k + 1) for k, send in enumerate(branch_sends)]
    gate_up_split = jnp.transpose(gate_up, (1, 0, 2))
    middle = hidden_units // 2
    dp_index = lax.axis_index(DP)
    dp_count = lax.axis_size(DP)

    def own_rows(source, axis_dim):
        length = source.shape[axis_dim] // dp_count
        return lax.dynamic_slice_in_dim(source, dp_index * length, length, axis_dim)

    own_weights = (
        own_rows(query_key, 0).astype(F32),
        own_rows(value_gate, 0).astype(F32),
        own_rows(output_weight, 1).astype(F32),
        own_rows(gate_up, 0).astype(F32),
        own_rows(down_weight, 1).astype(F32),
    )
    own_weights, branch_keep = lax.optimization_barrier((own_weights, branch_keep))
    own_query_key, own_value_gate, own_output_weight, own_gate_up, own_down_weight = own_weights
    hidden_own = inputs_turned.astype(F32) + branch_keep
    for piece in arrived:
        hidden_own = hidden_own + piece.astype(F32)
    hidden = lax.all_gather(hidden_own.astype(BF), TENSOR, axis=0, tiled=True)

    cot_turned, normed_two_turned, root_two, ffn_right, keep_two, *sends_two = pl.pallas_call(
        ffn_kernel,
        out_shape=[
            shaped(width, tokens, dtype=BF),
            shaped(width, tokens, dtype=BF),
            shaped(8, tokens),
            shaped(3, tokens, hidden_units, dtype=BF),
            shaped(share, tokens),
        ]
        + sends(),
        in_specs=[scalars()] + [vmem] * (4 + groups),
        scratch_shapes=[pltpu.VMEM((tokens, width), BF), pltpu.VMEM((width, tokens), F32)],
        cost_estimate=cost(10 * tokens * width * hidden_units, 6 * width * hidden_units),
        name="ffn",
    )(own_index, hidden, gain_columns, gate_up_split, down_weight, *cot_pieces)
    arrived_two = [swap_tensor(send, k + 1) for k, send in enumerate(sends_two)]

    middle = hidden_units // 2
    ffn_pairs = [(each, swap_dp(each, 0)) for each in (normed_two_turned, cot_turned, ffn_right)]
    ffn_group = (ffn_pairs[:2], ffn_pairs[2], hidden_units // 2)
    ffn_sends = sum_rows(*ffn_group, False)
    ffn_keeps = sum_rows(*ffn_group, True)

    d_normed_two_own, d_normed_two_rounded = pl.pallas_call(
        lambda *refs: add_kernel(groups, *refs),
        out_shape=[shaped(share, tokens), shaped(share, tokens, dtype=BF)],
        in_specs=[vmem] * groups + [pl.BlockSpec(memory_space=pl.ANY)] * 2,
        cost_estimate=cost(4 * share * tokens, 14 * share * tokens),
        name="add",
    )(keep_two, *arrived_two, *ffn_sends)
    d_normed_two_pieces = [d_normed_two_rounded] + [
        swap_tensor(d_normed_two_rounded, k) for k in range(1, groups)
    ]
    ffn_rows = sum_rows_third(ffn_sends, ffn_keeps)
    feed_keep, *feed_sends = pl.pallas_call(
        feed_kernel,
        out_shape=[shaped(share, tokens)] + sends(),
        grid=(1,),
        in_specs=[
            scalars(),
            pl.BlockSpec((1, tokens, hidden_units), lambda k: (2, 0, 0)),
            pl.BlockSpec((hidden_units, width), lambda k: (0, 0)),
        ],
        out_specs=[pl.BlockSpec((share, tokens), lambda k: (0, 0))] * groups,
        scratch_shapes=[pltpu.VMEM((width, tokens), F32)],
        cost_estimate=cost(2 * tokens * width * hidden_units, 2 * width * hidden_units),
        name="feed",
    )(own_index, ffn_right, down_weight)

    d_hidden_own, d_branch_turned, delta, taps_part, keep_one, line_one, *sends_one = (
        pl.pallas_call(
            back_kernel,
            out_shape=[
                shaped(share, tokens),
                shaped(width, tokens, dtype=BF),
                shaped(1, tokens, 3 * (share + key_width), dtype=BF),
                shaped(8, share),
                shaped(share, tokens),
                shaped(8, tokens),
            ]
            + sends(EXTRA),
            in_specs=[scalars()] + [vmem] * (16 + groups),
            scratch_shapes=[
                pltpu.VMEM((width, tokens), F32),
                pltpu.VMEM((tokens, width), BF),
                pltpu.VMEM((tokens + 16, share), F32),
                pltpu.VMEM((tokens, share), F32),
                pltpu.VMEM((width, tokens), BF),
            ],
            cost_estimate=cost(8 * tokens * width * share, 20 * width * share),
            name="back",
        )(
            own_index, hidden, root_two, gain_columns, cot_turned, x_turned,
            root_one, output_weight, projected, mixing, attended, mixed_values, conv_taps, lines,
            query_key_rows, value_gate_rows, gated, *d_normed_two_pieces,
        )
    )
    arrived_one = [swap_tensor(send, k + 1) for k, send in enumerate(sends_one)]
    all_columns = 2 * (share + key_width)
    mix_pairs = [normed_pair] + [(each, swap_dp(each, 0)) for each in (d_branch_turned, delta)]
    mix_group = (mix_pairs[:2], mix_pairs[2], all_columns // 4)
    mix_sends = sum_rows(*mix_group, False)
    mix_keeps = sum_rows(*mix_group, True)
    mix_rows = sum_rows_third(mix_sends, mix_keeps)

    feed_own = feed_keep
    feed_arrived = [swap_tensor(send, k + 1) for k, send in enumerate(feed_sends)]
    for piece in feed_arrived:
        feed_own = feed_own + piece.astype(F32)
    mixed = (hidden_own + feed_own).astype(BF).T

    def own_rows_of(source):
        return lax.dynamic_slice_in_dim(source, own * share, share, 0)

    gain_own = gains.astype(F32).T
    root_one_line, root_two_line = root_one[0:1], root_two[0:1]
    unit_two_own = own_rows_of(hidden).astype(F32) * root_two_line
    gain_two_grad = jnp.sum(d_normed_two_own * unit_two_own, axis=1)
    d_normed_own, line = keep_one, line_one[0:1]
    for piece in arrived_one:
        d_normed_own = d_normed_own + piece[:share].astype(F32)
        line = line + (piece[share : share + 1].astype(F32) + piece[share + 1 : share + 2].astype(F32))
    unit_one_own = inputs_turned.astype(F32) * root_one_line
    input_grad = (
        d_hidden_own
        + root_one_line * (d_normed_own * gain_own[:, 0:1] - unit_one_own * (line / width))
    ).T
    gain_one_grad = jnp.sum(d_normed_own * unit_one_own, axis=1)
    small = sum_dp(
        jnp.concatenate(
            [gain_one_grad[None], gain_two_grad[None], taps_part[:KERNEL], jnp.zeros((2, share))],
            axis=0,
        )
    )
    gains_grad = small[:2]
    conv_taps_grad = small[2 : 2 + KERNEL]
    down_weight_grad = sum(part[:, middle:].astype(F32) for part in ffn_rows[1]).T
    down_weight_grad = with_layout_constraint(
        lax.optimization_barrier(down_weight_grad), Layout(major_to_minor=(1, 0))
    )
    rows = width // lax.axis_size(DP)

    def turned_pairs(source):
        return source.transpose(1, 2, 0).reshape(2 * key_width, rows)

    last = pl.pallas_call(
        lambda *refs: last_kernel(share, 2 * key_width, *refs),
        out_shape=[shaped(rows, 2, share)] * 4
        + [shaped(2 * key_width, rows)] * 4
        + [shaped(share, rows)] * 4,
        in_specs=[vmem] * 13,
        scratch_shapes=[pltpu.VMEM((rows, 3 * (share + key_width)), F32)],
        cost_estimate=cost(30 * rows * share, 100 * rows * share),
        name="last",
    )(
        *mix_rows[0], *mix_rows[1],
        own_value_gate, value_gate_moment, value_gate_mean,
        turned_pairs(own_query_key), turned_pairs(query_key_moment),
        turned_pairs(probe_lookup_smoothed),
        own_output_weight, output_weight_moment, output_weight_mean,
    )
    value_gate_grad, value_gate_change, value_gate_momentum, value_gate_average = last[:4]
    query_key_grad, query_key_change, query_key_momentum, query_key_average = [
        each.reshape(2, key_width, rows).transpose(2, 0, 1) for each in last[4:8]
    ]
    (
        output_weight_grad, output_weight_change, output_weight_momentum,
        output_weight_average,
    ) = last[8:]
    gains_change, gains_momentum, gains_average = advance(
        gains_grad, gains, gains_moment, gains_mean
    )
    conv_taps_change, conv_taps_momentum, conv_taps_average = advance(
        conv_taps_grad, conv_taps, conv_taps_moment, conv_taps_mean
    )
    gate_up_grad, gate_up_change, gate_up_momentum, gate_up_average = advance_pairs(
        *ffn_rows, middle, own_gate_up, gate_up_moment, gate_up_mean
    )
    down_weight_change, down_weight_momentum, down_weight_average = advance(
        down_weight_grad, own_down_weight, down_weight_moment, down_weight_mean
    )
    return (
        mixed,
        input_grad,
        gains_grad,
        query_key_grad,
        value_gate_grad,
        conv_taps_grad,
        output_weight_grad,
        gate_up_grad,
        down_weight_grad,
        gains_change,
        query_key_change,
        value_gate_change,
        conv_taps_change,
        output_weight_change,
        gate_up_change,
        down_weight_change,
        gains_momentum,
        query_key_momentum,
        value_gate_momentum,
        conv_taps_momentum,
        output_weight_momentum,
        gate_up_momentum,
        down_weight_momentum,
        gains_average,
        query_key_average,
        value_gate_average,
        conv_taps_average,
        output_weight_average,
        gate_up_average,
        down_weight_average,
    )


def solution(mesh):
    return jax.shard_map(
        local,
        mesh=mesh,
        in_specs=(
            P(DP, TENSOR),
            P(DP, TENSOR),
            P(DP),
            P(None, TENSOR),
            P(None, None, TENSOR),
            P(None, None, TENSOR),
            P(None, TENSOR),
            P(TENSOR, None),
            P(None, None, TENSOR),
            P(TENSOR, None),
            P(None, TENSOR),
            P(DP, None, TENSOR),
            P(DP, None, TENSOR),
            P(None, TENSOR),
            P(TENSOR, DP),
            P(DP, None, TENSOR),
            P(TENSOR, DP),
            P(None, TENSOR),
            P(DP, None, TENSOR),
            P(DP, None, TENSOR),
            P(None, TENSOR),
            P(TENSOR, DP),
            P(DP, None, TENSOR),
            P(TENSOR, DP),
        ),
        out_specs=(
            P(DP, TENSOR),
            P(DP, TENSOR),
            P(None, TENSOR),
            P(DP, None, TENSOR),
            P(DP, None, TENSOR),
            P(None, TENSOR),
            P(TENSOR, DP),
            P(DP, None, TENSOR),
            P(TENSOR, DP),
            P(None, TENSOR),
            P(DP, None, TENSOR),
            P(DP, None, TENSOR),
            P(None, TENSOR),
            P(TENSOR, DP),
            P(DP, None, TENSOR),
            P(TENSOR, DP),
            P(None, TENSOR),
            P(DP, None, TENSOR),
            P(DP, None, TENSOR),
            P(None, TENSOR),
            P(TENSOR, DP),
            P(DP, None, TENSOR),
            P(TENSOR, DP),
            P(None, TENSOR),
            P(DP, None, TENSOR),
            P(DP, None, TENSOR),
            P(None, TENSOR),
            P(TENSOR, DP),
            P(DP, None, TENSOR),
            P(TENSOR, DP),
        ),
        check_vma=False,
    )
```
